512 devices in a mesh: seq: 64 (over y, z), chan: 8 (over x, core).
Axes of the slice: x: 4, y: 8, z: 8, core: 2. Of those that a mesh axis runs over, the one named last changes fastest.
Arguments:
- query_rows: bfloat16 [24576, 8192], P('seq', 'chan'), may hold values from -6 to 6
- key_rows: bfloat16 [24576, 8192], P('seq', 'chan'), may hold values from -6 to 6
- value_rows: bfloat16 [24576, 8192], P('seq', 'chan'), may hold values from -6 to 6
- residues: float32 [512, 16], P('chan'), may hold values from -9.2 to 9.2
- decay_rates: float32 [512, 16], P('chan'), may hold values from 1.9938151e-06 to 0.0334
- medium_taps: float32 [512, 128], P('chan'), may hold values from -0.5 to 0.5
- out_gain: float32 [8192], P('chan'), may hold values from 0.1 to 1.9
- reader_plan: int32 [512, 9], P('chan'), may hold values from 0 to 63, as said below
Outputs:
- mixed: bfloat16 [24576, 8192], P('seq', 'chan')
- handoff: float32 [640, 16, 128], P('seq', None, 'chan')
The draws below stay inside these ranges and needn't reach their ends.
Inputs may be any that keep to these rules, and one draw needn't show every extreme that they name: `reader_plan`: each row names 9 different readers. Within each aligned block of 64 filters (the rows of one device along chan) every reader appears at least once, none more than 10 times, and one reader exactly 10 times.
All inputs are finite; a program needn't handle non-finite values.
Results may differ from the reference program's by a relative error of at most 0.0049.
Values may be sent and summed in bfloat16 or wider, within the bound.
A program may use at most 128 MiB of HBM per device.

```python
import jax
import jax.numpy as jnp
from jax import lax

D = 8192
GW = 16
MODES = 16
MED = 128
SEQLEN = 24576
FILTERS = 512
GPD = 64
NB = 8
CAP = 10
N_SEQ = 64
N_CHAN = 8


def draw_residues(key, part):
    ramp = jnp.arange(FILTERS).astype(jnp.float32) / max(FILTERS - 1, 1)
    values = jnp.clip(jax.random.normal(key, (FILTERS, MODES), jnp.float32), -4.0, 4.0)
    rising = jnp.exp(jnp.log(3.0) * ramp)
    return 0.6 * values * rising[:, None]


def draw_decay_rates(key, part):
    key_one, key_two, key_three = jax.random.split(key, 3)
    share = 0.5
    slow = jax.random.uniform(key_one, (FILTERS, MODES), jnp.float32) < share
    slow_rate = jnp.exp(jax.random.uniform(key_two, (FILTERS, MODES), jnp.float32, jnp.log(0.05 / SEQLEN), jnp.log(2.0 / SEQLEN)))
    fast_rate = jnp.exp(jax.random.uniform(key_three, (FILTERS, MODES), jnp.float32, jnp.log(1.0 / 50.0), jnp.log(1.0 / 30.0)))
    return jnp.where(slow, slow_rate, fast_rate)


def plan_block(block_key):
    perm_key, shift_key = jax.random.split(block_key, 2)
    order = jax.random.permutation(perm_key, N_SEQ).astype(jnp.int32)
    offset = jax.random.randint(shift_key, (), 0, N_SEQ - 1).astype(jnp.int32)
    hot = order[0]
    others = order[1:]
    rows = jnp.arange(GPD).astype(jnp.int32)[:, None]
    cols = jnp.arange(NB + 1).astype(jnp.int32)[None, :]
    index = rows * (NB + 1) + cols
    is_hot = (rows < CAP) & (cols == 0)
    before = jnp.minimum(rows, CAP) + ((cols > 0) & (rows < CAP)).astype(jnp.int32)
    counter = index - before
    pick = (counter + offset) % (N_SEQ - 1)
    return jnp.where(is_hot, hot, others[pick]).astype(jnp.int32)


def draw_reader_plan(key, part):
    block_keys = jax.random.split(jax.random.fold_in(key, 7), FILTERS // GPD)
    blocks = jax.vmap(plan_block)(block_keys)
    return blocks.reshape(FILTERS, NB + 1)


def levels(rng, dims, pieces, smallest, top_value):
    gain, own = 1.0, jax.random.fold_in(rng, 6)
    for position, parts in pieces:
        heights = jnp.exp(jax.random.uniform(jax.random.fold_in(own, position), (parts,), jnp.float32, smallest / len(pieces), top_value / len(pieces)))
        gain = gain * jnp.repeat(heights, dims[position] // parts).reshape([-1 if axis == position else 1 for axis in range(len(dims))])
    return gain


def centred(rng, extent, spread, reach, cuts=(), kind=jnp.bfloat16):
    gain = levels(rng, extent, cuts, -0.22, 0.18) if cuts else 1.0
    entries = jax.random.normal(rng, extent, jnp.float32) * spread * gain
    return jnp.minimum(jnp.maximum(entries, -reach), reach).astype(kind)


def setup_inputs(seed: int = 0) -> dict:
    keys = jax.random.split(jax.random.key(seed), 9)
    query_rows = centred(keys[0], (SEQLEN, D), 1.0, 6.0, ((0, 64), (1, 8)))
    key_rows = centred(keys[1], (SEQLEN, D), 1.0, 6.0, ((0, 64), (1, 8)))
    value_rows = centred(keys[2], (SEQLEN, D), 1.0, 6.0, ((0, 64), (1, 8)))
    residues = draw_residues(jax.random.fold_in(keys[8], 71), 0)
    decay_rates = draw_decay_rates(jax.random.fold_in(keys[8], 71), 0)
    medium_taps = centred(keys[5], (FILTERS, MED), MED ** -0.5, 0.5, ((0, 8),), jnp.float32)
    out_gain = jnp.clip(1.0 + 0.18 * jax.random.normal(keys[6], (D,), jnp.float32), 0.1, 1.9)
    reader_plan = draw_reader_plan(jax.random.fold_in(keys[8], 71), 0)
    return dict(query_rows=query_rows, key_rows=key_rows, value_rows=value_rows, residues=residues, decay_rates=decay_rates, medium_taps=medium_taps, out_gain=out_gain, reader_plan=reader_plan)


def reference(query_rows, key_rows, value_rows, residues, decay_rates, medium_taps, out_gain, reader_plan):
    highest = lax.Precision.HIGHEST
    product = (key_rows.astype(jnp.float32) * value_rows.astype(jnp.float32)).astype(jnp.bfloat16)
    norm_factor = jnp.sqrt(-jnp.expm1(-2.0 * decay_rates))
    positions = jnp.arange(SEQLEN).astype(jnp.float32)
    grouped = product.reshape(SEQLEN, FILTERS, GW).transpose(1, 0, 2)
    queries = query_rows.reshape(SEQLEN, FILTERS, GW).transpose(1, 0, 2)

    def per_filter(operands):
        rows, query_part, coeffs, rates, taps, factor = operands
        rows = rows.astype(jnp.float32)
        decays = jnp.exp(-rates[:, None] * positions[None, :])
        response = jnp.dot(coeffs * factor, decays, precision=highest) + jnp.pad(taps, (0, SEQLEN - MED))
        length = 2 * SEQLEN
        spectrum = jnp.fft.rfft(response, length)[:, None] * jnp.fft.rfft(rows, length, axis=0)
        conv = jnp.fft.irfft(spectrum, length, axis=0)[:SEQLEN].astype(jnp.float32)
        gated = query_part.astype(jnp.float32) * conv
        ends = jnp.exp(-rates[:, None] * (SEQLEN - positions)[None, :])
        state = factor[:, None] * jnp.dot(ends, rows, precision=highest)
        tail = rows[SEQLEN - MED:].reshape(NB, MODES, GW)
        items = jnp.concatenate([tail, state[None]], axis=0)
        return (gated, items)
    gated, items = lax.map(per_filter, (grouped, queries, residues, decay_rates, medium_taps, norm_factor))
    energy = lax.optimization_barrier(jnp.sum(lax.optimization_barrier(jnp.sum(gated * gated, axis=2)), axis=0))
    scale = lax.rsqrt(energy / D + 1e-05)
    gated = gated.transpose(1, 0, 2).reshape(SEQLEN, D)
    mixed = (gated * scale[:, None] * out_gain[None, :]).astype(jnp.bfloat16)
    flat_items = items.reshape(N_CHAN, GPD * (NB + 1), MODES * GW)
    plan_blocks = reader_plan.reshape(N_CHAN, GPD * (NB + 1))
    readers = jnp.arange(N_SEQ).astype(jnp.int32)
    chosen = plan_blocks[:, None, :] == readers[None, :, None]
    ranks = jnp.cumsum(chosen.astype(jnp.int32), axis=2) - 1
    slots = jnp.arange(CAP).astype(jnp.int32)
    select = (chosen[:, :, None, :] & (ranks[:, :, None, :] == slots[None, None, :, None])).astype(jnp.float32)
    handoff = jnp.einsum('nrji,nip->nrjp', select, flat_items.astype(jnp.float32), precision=highest)
    handoff = handoff.reshape(N_CHAN, N_SEQ * CAP, MODES, GW).transpose(1, 2, 0, 3).reshape(N_SEQ * CAP, MODES, N_CHAN * GW)
    return (mixed, handoff)
```

```python
import functools
import math

import jax
import jax.numpy as jnp
from jax import lax
from jax.experimental import pallas as pl
from jax.experimental.pallas import tpu as pltpu
from jax.sharding import PartitionSpec as P

D = 8192
GW = 16
MODES = 16
MED = 128
NB = 8
SLOTS = 16
LANES = 128
F32 = jnp.float32
BF16 = jnp.bfloat16
MESH = pl.DeviceIdType.MESH


def iota(shape, axis):
    return lax.broadcasted_iota(jnp.int32, shape, axis)


def split(x, parts):
    out = []
    for _ in range(parts):
        piece = x.astype(BF16)
        out.append(piece)
        x = x - piece.astype(F32)
    return out


def one_minus_exp_neg(x):
    small = x * (1.0 - x * (1 / 2) * (1.0 - x * (1 / 3) * (1.0 - x * (1 / 4) * (
        1.0 - x * (1 / 5) * (1.0 - x * (1 / 6) * (1.0 - x * (1 / 7)))))))
    return jnp.where(x < 0.1, small, 1.0 - jnp.exp(-x))


def dot(a, b):
    return jnp.dot(a, b, preferred_element_type=F32)


def swap_blocks(x):
    n = x.shape[0]
    sub = iota((n, 8, LANES), 1)
    blk = iota((n, 8, LANES), 2) // GW
    gap = (blk - sub + 8) % 8
    out = x
    for d in range(1, 8):
        moved = pltpu.roll(pltpu.roll(x, 8 - d, 1), GW * d, 2)
        out = jnp.where(gap == d, moved, out)
    return out


def kernel(cfg, q_hbm, k_hbm, v_hbm, res_ref, lam_ref, taps_ref, gain_ref, plan_ref,
           out_hbm, hand_ref,
           kbuf, vbuf, qbuf, xbuf, hbuf, lamc, wc, eb, lame, gh, gt, tmat, smat, rhs, local, st,
           a1s, a1r, pre, a2s, a2r, a3s, a3r, items, pk, row, tin, es, er, obuf,
           in_sem, out_sem, s1, r1, s2, r2, s3, r3, sx, rx, sh, rh, sp, rp, sf, rf):
    ny, nz, nc, tiles, tokens = cfg
    groups = tiles * 8
    chunks = tokens // MED
    me = lax.axis_index("seq")
    ch = lax.axis_index("chan")
    y = me // nz
    z = me % nz
    last = ny * nz - 1

    for c in range(chunks):
        rows = pl.ds(c * MED, MED)
        pltpu.make_async_copy(k_hbm.at[rows], kbuf.at[rows], in_sem.at[0, c]).start()
        pltpu.make_async_copy(v_hbm.at[rows], vbuf.at[rows], in_sem.at[1, c]).start()
    pltpu.make_async_copy(q_hbm, qbuf, in_sem.at[2, 0]).start()

    barrier = pltpu.get_barrier_semaphore()

    def greet(seq, chan):
        pl.semaphore_signal(barrier, inc=1, device_id=(seq, chan), device_id_type=MESH)

    for d in range(1, nz):
        greet(y * nz + (z + d) % nz, ch)
    for d in range(1, ny):
        greet(((y + d) % ny) * nz + z, ch)
    for d in range(1, nc):
        greet(me, (ch + d) % nc)
    wraps_on = (z == nz - 1) & (y < ny - 1)
    wraps_in = (z == 0) & (y > 0)

    @pl.when(wraps_on)
    def _():
        greet(me + 1, ch)

    @pl.when(wraps_in)
    def _():
        greet(me - 1, ch)

    lam_t = jnp.transpose(lam_ref[...])
    res_t = jnp.transpose(res_ref[...])
    lane16 = iota((MODES, LANES), 1) // GW
    lane128 = iota((LANES, LANES), 1)
    back = (LANES - lane128).astype(F32)
    for g in range(tiles):
        spread = jnp.zeros((MODES, LANES), F32)
        cols = []
        rescols = []
        for k in range(8):
            f = g * 8 + k
            col = jnp.broadcast_to(lam_t[:, f:f + 1], (MODES, LANES))
            cols.append(col)
            rescols.append(jnp.broadcast_to(res_t[:, f:f + 1], (MODES, LANES)))
            spread = jnp.where(lane16 == k, col, spread)
        lame[:, g * LANES:(g + 1) * LANES] = spread
        rates = jnp.concatenate(cols, axis=0)
        lamc[g * LANES:(g + 1) * LANES, :] = rates
        weight = jnp.concatenate(rescols, axis=0) * jnp.sqrt(one_minus_exp_neg(2.0 * rates))
        wc[g * LANES:(g + 1) * LANES, :] = weight
        e = jnp.exp(-rates * back)
        hi, lo = split(e, 2)
        eb[g, 0:LANES, :] = hi
        eb[g, LANES:2 * LANES, :] = lo
        modal = jnp.where(lane128 == 0, weight, weight * e)
        gh[g * 8:(g + 1) * 8, :] = jnp.sum(modal.reshape(8, MODES, LANES), axis=1)

    for c in range(chunks):
        rows = pl.ds(c * MED, MED)
        pltpu.make_async_copy(k_hbm.at[rows], kbuf.at[rows], in_sem.at[0, c]).wait()
        pltpu.make_async_copy(v_hbm.at[rows], vbuf.at[rows], in_sem.at[1, c]).wait()
        xbuf[rows, :] = (kbuf[rows, :].astype(F32) * vbuf[rows, :].astype(F32)).astype(BF16)

    own16 = iota((MODES, LANES), 1) // GW
    for g in range(tiles):
        lanes = slice(g * LANES, (g + 1) * LANES)
        total = None
        d128 = jnp.exp(lame[:, lanes] * (-float(MED)))
        both = [xbuf[c * MED:(c + 1) * MED, lanes] for c in range(chunks)]
        raw = dot(eb[g], jnp.concatenate(both, axis=1))
        raw = raw[0:LANES] + raw[LANES:2 * LANES]
        for c in range(chunks):
            part = jnp.zeros((MODES, LANES), F32)
            for k in range(8):
                piece = raw[k * MODES:(k + 1) * MODES, c * LANES:(c + 1) * LANES]
                part = jnp.where(own16 == k, piece, part)
            total = part if total is None else total * d128 + part
            if c < chunks - 1:
                st[c, :, lanes] = total
        a1s[g] = total.astype(BF16)

    extra = wraps_on.astype(jnp.int32) + wraps_in.astype(jnp.int32)
    pl.semaphore_wait(barrier, (nz - 1) + (ny - 1) + (nc - 1) + extra)

    def remote(src, dst, send, recv, seq, chan):
        return pltpu.make_async_remote_copy(
            src_ref=src, dst_ref=dst, send_sem=send, recv_sem=recv,
            device_id=(seq, chan), device_id_type=MESH)

    def order(n):
        return sorted(range(1, n), key=lambda d: -min(d, n - d))

    sent1 = []
    for d in order(nz):
        to = (z + d) % nz
        copy = remote(a1s.at[to], a1r.at[z], s1.at[d], r1.at[z], y * nz + to, ch)
        copy.start()
        sent1.append(copy)
    a1r[z] = a1s[z]

    def halo():
        return remote(xbuf.at[pl.ds(tokens - MED, MED)], hbuf, sh, rh, me + 1, ch)

    @pl.when(me < last)
    def _():
        halo().start()

    plan = plan_ref[...]
    tri = (iota((groups, groups), 1) < iota((groups, groups), 0)).astype(BF16)

    @pl.when(me == last)
    def _():
        who = iota((groups, LANES), 1)
        hits = jnp.zeros((groups, LANES), F32)
        for b in range(NB + 1):
            hits = hits + (plan[:, b:b + 1] == who).astype(F32)
        before = dot(tri, hits.astype(BF16))
        slots = jnp.full((groups, LANES), -1.0, F32)
        for b in range(NB):
            reader = plan[:, b:b + 1]
            rank = jnp.sum(jnp.where(reader == who, before, 0.0), axis=1, keepdims=True)
            slot = reader.astype(F32) * SLOTS + rank
            slots = jnp.where(who == b, slot, slots)
        slots_t = jnp.transpose(slots)
        for b in range(NB):
            for half in range(2):
                first = tokens - MED + b * MODES + half * 8
                for g in range(tiles):
                    tile = xbuf[tokens - MED + b * MODES:tokens - MED + (b + 1) * MODES,
                                g * LANES:(g + 1) * LANES].astype(F32)[half * 8:half * 8 + 8]
                    items[b * groups + g * 8:b * groups + g * 8 + 8,
                          half * LANES:(half + 1) * LANES] = swap_blocks(tile[None])[0]
        for part in range(ny):
            count = nz * SLOTS
            base = part * count
            acc = jnp.zeros((count, 2 * LANES), F32)
            for b in range(NB):
                target = (iota((count, groups), 0) + base).astype(F32)
                pick = (target == slots_t[b:b + 1, 0:groups]).astype(BF16)
                acc = acc + dot(pick, items[b * groups:(b + 1) * groups, :].astype(BF16))
            packed = acc.astype(BF16).reshape(nz, SLOTS, 2 * LANES)
            if part == ny - 1:
                row[...] = packed
            else:
                pk[part] = packed

    def pack_copy(part):
        return remote(pk.at[part], row, sp.at[part], rp, part * nz + nz - 1, ch)

    @pl.when(me == last)
    def _():
        for part in range(ny - 1):
            pack_copy(part).start()

    perm = (iota((LANES, LANES), 0) == (LANES - iota((LANES, LANES), 1)) % LANES).astype(BF16)
    flipped = dot(jnp.concatenate(split(taps_ref[...], 3), axis=0), perm)
    flipped = flipped[0:groups] + flipped[groups:2 * groups] + flipped[2 * groups:3 * groups]
    gt[...] = flipped
    gh[...] = gh[...] + flipped

    def conv_tile(g, carry):
        lanes = pl.ds(pl.multiple_of(g * LANES, LANES), LANES)
        rows8 = pl.ds(pl.multiple_of(g * 8, 8), 8)
        full = gh[rows8, :]
        taps = gt[rows8, :]
        lower = iota((LANES, LANES), 1) <= iota((LANES, LANES), 0)
        which = iota((MED, LANES), 1) // GW
        x0 = xbuf[0:MED, lanes]
        x1 = xbuf[MED:2 * MED, lanes]
        x2 = xbuf[2 * MED:3 * MED, lanes]
        for k in range(8):
            a = pltpu.roll(jnp.broadcast_to(full[k:k + 1], (LANES, LANES)), 0, 1, stride=1, stride_axis=0)
            b = pltpu.roll(jnp.broadcast_to(taps[k:k + 1], (LANES, LANES)), 0, 1, stride=1, stride_axis=0)
            cols = slice(k * LANES, (k + 1) * LANES)
            tmat[g, 0:LANES, cols] = jnp.where(lower, a, 0.0).astype(BF16)
            tmat[g, LANES:2 * LANES, cols] = jnp.where(lower, 0.0, b).astype(BF16)
            keep = (which == k).astype(BF16)
            rhs[cols, 0:LANES] = x0 * keep
            rhs[cols, LANES:2 * LANES] = x1 * keep
            rhs[cols, 2 * LANES:3 * LANES] = x2 * keep
        out = dot(tmat[g], rhs[:, 0:2 * LANES])
        out2 = dot(tmat[g, 0:LANES, :], rhs[:, 2 * LANES:3 * LANES])
        local[0:MED, lanes] = out[0:LANES, 0:LANES]
        local[MED:2 * MED, lanes] = out[0:LANES, LANES:2 * LANES] + out[LANES:2 * LANES, 0:LANES]
        local[2 * MED:3 * MED, lanes] = out2 + out[LANES:2 * LANES, LANES:2 * LANES]
        return carry

    lax.fori_loop(0, tiles, conv_tile, 0)

    mine = pl.ds(pl.multiple_of(z * LANES, LANES), LANES)
    lam_s = lame[:, mine]
    d_dev = jnp.exp(lam_s * (-float(tokens)))
    for d in range(1, nz):
        frm = (z - d + nz) % nz
        remote(a1s.at[0], a1r.at[frm], s1.at[d], r1.at[frm], me, ch).wait_recv()
    run = jnp.zeros((MODES, LANES), F32)
    for i in range(nz):
        pre[i] = run
        run = run * d_dev + a1r[i].astype(F32)
    a2s[...] = run.astype(BF16)

    sent2 = []
    for d in order(ny):
        to = (y + d) % ny
        copy = remote(a2s, a2r.at[y], s2.at[d], r2.at[y], to * nz + z, ch)
        copy.start()
        sent2.append(copy)
    a2r[y] = a2s[...]

    def carry_tile(g, carry):
        lanes = pl.ds(pl.multiple_of(g * LANES, LANES), LANES)
        rates = lamc[lanes, :]
        weight = wc[lanes, :]
        at = lane128.astype(F32)
        for c in range(chunks):
            s = weight * jnp.exp(-rates * (at + float(c * MED)))
            smat[c * MED:(c + 1) * MED, lanes] = jnp.transpose(s).astype(BF16)
        same = (iota((LANES, LANES), 0) // MODES) == (iota((LANES, LANES), 1) // GW)
        pieces = []
        for c in range(chunks - 1):
            state = jnp.concatenate([st[c, :, lanes]] * 8, axis=0)
            pieces.append(jnp.where(same, state, 0.0))
        hi, lo = split(jnp.concatenate(pieces, axis=1), 2)
        factor = smat[0:MED, lanes]
        out = dot(factor, hi) + dot(factor, lo)
        for c in range(chunks - 1):
            rows = slice((c + 1) * MED, (c + 2) * MED)
            local[rows, lanes] = local[rows, lanes] + out[:, c * LANES:(c + 1) * LANES]
        return carry

    lax.fori_loop(0, tiles, carry_tile, 0)

    d_row = jnp.exp(lam_s * (-float(tokens * nz)))
    for d in range(1, ny):
        frm = (y - d + ny) % ny
        remote(a2s, a2r.at[frm], s2.at[d], r2.at[frm], me, ch).wait_recv()
    run = jnp.zeros((MODES, LANES), F32)
    above = jnp.zeros((MODES, LANES), F32)
    for i in range(ny):
        above = jnp.where(y == i, run, above)
        run = run * d_row + a2r[i].astype(F32)
    norm_s = jnp.sqrt(one_minus_exp_neg(2.0 * lam_s))
    final = (run * norm_s).astype(BF16)
    for i in range(nz):
        a3s[i, 0] = (above + pre[i]).astype(BF16)
        a3s[i, 1] = final
        above = above * d_dev

    sent3 = []
    for d in order(nz):
        to = (z + d) % nz
        copy = remote(a3s.at[to], a3r.at[z], s3.at[d], r3.at[z], y * nz + to, ch)
        copy.start()
        sent3.append(copy)
    a3r[z] = a3s[z]

    def hop_copy(to):
        return remote(row.at[to], tin, sf.at[to], rf, y * nz + to, ch)

    @pl.when((z == nz - 1) & (me != last))
    def _():
        remote(pk.at[0], row, sp.at[0], rp, me, ch).wait_recv()

    @pl.when(z == nz - 1)
    def _():
        for to in range(nz - 1):
            hop_copy(to).start()
        tin[...] = row[nz - 1]

    @pl.when(me > 0)
    def _():
        remote(xbuf.at[pl.ds(tokens - MED, MED)], hbuf, sh, rh, me, ch).wait_recv()

        def halo_tile(g, carry):
            lanes = pl.ds(pl.multiple_of(g * LANES, LANES), LANES)
            which = iota((MED, LANES), 1) // GW
            xh = hbuf[:, lanes]
            for k in range(8):
                rhs[k * LANES:(k + 1) * LANES, 0:LANES] = xh * (which == k).astype(BF16)
            out = dot(tmat[g, LANES:2 * LANES, :], rhs[:, 0:LANES])
            local[0:MED, lanes] = local[0:MED, lanes] + out
            return carry

        lax.fori_loop(0, tiles, halo_tile, 0)

    pltpu.make_async_copy(q_hbm, qbuf, in_sem.at[2, 0]).wait()
    for d in range(1, nz):
        frm = (z - d + nz) % nz
        remote(a3s.at[0], a3r.at[frm], s3.at[d], r3.at[frm], me, ch).wait_recv()

    power = jnp.zeros((tokens, LANES), F32)
    wide = 2 * LANES
    same2 = ((iota((wide, wide), 0) // MODES) == (iota((wide, wide), 1) // GW)).astype(BF16)
    for g in range(tiles // 2):
        lanes = slice(g * wide, (g + 1) * wide)
        state = jnp.concatenate([a3r[2 * g, 0], a3r[2 * g + 1, 0]], axis=1)
        spread = jnp.concatenate([state] * 16, axis=0) * same2
        cross = dot(smat[:, lanes], spread)
        gated = qbuf[:, lanes].astype(F32) * (local[:, lanes] + cross)
        local[:, lanes] = gated
        sq = gated * gated
        power = power + sq[:, 0:LANES] + sq[:, LANES:wide]
    es[...] = jnp.sum(jnp.transpose(power), axis=0, keepdims=True)

    sentx = []
    for d in order(nc):
        to = (ch + d) % nc
        copy = remote(es, er.at[ch], sx.at[d], rx.at[ch], me, to)
        copy.start()
        sentx.append(copy)
    er[ch] = es[...]

    mine_hit = (plan == me)
    hit = jnp.sum(mine_hit.astype(F32), axis=1, keepdims=True)
    before = dot(tri, jnp.broadcast_to(hit, (groups, 2 * LANES)).astype(BF16))
    slot = (iota((groups, 2 * LANES), 1) // GW).astype(F32)
    wants = ((before == slot) & mine_hit[:, NB:NB + 1]).astype(BF16)
    picked = jnp.zeros((MODES, 2 * LANES), F32)
    delta = ((iota((LANES, 2 * LANES), 0) % GW) == (iota((LANES, 2 * LANES), 1) % GW)).astype(F32)
    for g in range(tiles):
        rep = ((iota((LANES, groups), 0) // GW + g * 8) == iota((LANES, groups), 1)).astype(BF16)
        choose = (dot(rep, wants) * delta).astype(BF16)
        picked = picked + dot(a3r[g, 1], choose)

    @pl.when(z != nz - 1)
    def _():
        remote(row.at[0], tin, sf.at[0], rf, me, ch).wait_recv()

    tails = tin[...].astype(F32)
    for a in range(2):
        for b in range(2):
            block = swap_blocks(tails[8 * a:8 * a + 8, b * LANES:(b + 1) * LANES][None])[0]
            block = block + picked[8 * b:8 * b + 8, a * LANES:(a + 1) * LANES]
            for k in range(8):
                j = a * 8 + k
                if j < 10:
                    hand_ref[j, 8 * b:8 * b + 8, :] = block[:, k * GW:(k + 1) * GW]

    for d in range(1, nc):
        frm = (ch - d + nc) % nc
        remote(es, er.at[frm], sx.at[d], rx.at[frm], me, ch).wait_recv()
    energy = er[0]
    for i in range(1, nc):
        energy = energy + er[i]
    scale = lax.rsqrt(energy / (nc * tiles * LANES) + 1e-05)
    scale = jnp.transpose(jnp.broadcast_to(scale, (LANES, tokens)))
    for c in range(chunks):
        rows = slice(c * MED, (c + 1) * MED)
        for g in range(tiles):
            lanes = slice(g * LANES, (g + 1) * LANES)
            obuf[rows, lanes] = (local[rows, lanes] * scale[rows] * gain_ref[:, lanes]).astype(BF16)
        pltpu.make_async_copy(obuf.at[rows], out_hbm.at[rows], out_sem.at[c]).start()

    for copy in sent1 + sent2 + sent3 + sentx:
        copy.wait_send()

    @pl.when(me < last)
    def _():
        halo().wait_send()

    @pl.when(me == last)
    def _():
        for part in range(ny - 1):
            pack_copy(part).wait_send()

    @pl.when(z == nz - 1)
    def _():
        for to in range(nz - 1):
            hop_copy(to).wait_send()

    for c in range(chunks):
        rows = slice(c * MED, (c + 1) * MED)
        pltpu.make_async_copy(obuf.at[rows], out_hbm.at[rows], out_sem.at[c]).wait()


def per_device(query_rows, key_rows, value_rows, residues, decay_rates, medium_taps, out_gain, reader_plan):
    tokens, channels = query_rows.shape
    tiles = channels // LANES
    groups = tiles * 8
    seq = lax.axis_size("seq")
    nz = math.isqrt(seq)
    ny = seq // nz
    nc = lax.axis_size("chan")
    cfg = (ny, nz, nc, tiles, tokens)
    chunks = tokens // MED
    vm = pltpu.VMEM
    dma = pltpu.SemaphoreType.DMA
    scratch = [
        vm((tokens, channels), BF16), vm((tokens, channels), BF16), vm((tokens, channels), BF16),
        vm((tokens, channels), BF16), vm((MED, channels), BF16),
        vm((channels, LANES), F32), vm((channels, LANES), F32), vm((tiles, 2 * LANES, LANES), BF16),
        vm((MODES, channels), F32), vm((groups, LANES), F32), vm((groups, LANES), F32),
        vm((tiles, 2 * LANES, 8 * LANES), BF16), vm((tokens, channels), BF16),
        vm((8 * LANES, 3 * LANES), BF16), vm((tokens, channels), F32),
        vm((chunks, MODES, channels), F32),
        vm((nz, MODES, LANES), BF16), vm((nz, MODES, LANES), BF16), vm((nz, MODES, LANES), F32),
        vm((MODES, LANES), BF16), vm((ny, MODES, LANES), BF16),
        vm((nz, 2, MODES, LANES), BF16), vm((nz, 2, MODES, LANES), BF16),
        vm((NB * groups, 2 * LANES), F32), vm((ny - 1, nz, SLOTS, 2 * LANES), BF16),
        vm((nz, SLOTS, 2 * LANES), BF16), vm((SLOTS, 2 * LANES), BF16),
        vm((1, tokens), F32), vm((nc, 1, tokens), F32), vm((tokens, channels), BF16),
        dma((3, chunks)), dma((chunks,)),
        dma((nz,)), dma((nz,)), dma((ny,)), dma((ny,)), dma((nz,)), dma((nz,)), dma((nc,)), dma((nc,)),
        dma, dma, dma((ny,)), dma, dma((nz,)), dma,
    ]
    hbm = pl.BlockSpec(memory_space=pl.ANY)
    vmem = pl.BlockSpec(memory_space=pltpu.VMEM)
    return pl.pallas_call(
        functools.partial(kernel, cfg),
        name="hyena",
        out_shape=(
            jax.ShapeDtypeStruct((tokens, channels), BF16),
            jax.ShapeDtypeStruct((10, MODES, GW), F32),
        ),
        in_specs=[hbm, hbm, hbm, vmem, vmem, vmem, vmem, vmem],
        out_specs=(hbm, vmem),
        scratch_shapes=scratch,
        compiler_params=pltpu.CompilerParams(
            collective_id=0, has_side_effects=True, vmem_limit_bytes=48 * 1024 * 1024),
    )(query_rows, key_rows, value_rows, residues, decay_rates, medium_taps,
      out_gain.reshape(1, channels), reader_plan)


def solution(mesh):
    placed = (
        P("seq", "chan"),
        P("seq", "chan"),
        P("seq", "chan"),
        P("chan", None),
        P("chan", None),
        P("chan", None),
        P("chan"),
        P("chan", None),
    )
    return jax.shard_map(
        per_device,
        mesh=mesh,
        in_specs=placed,
        out_specs=(P("seq", "chan"), P("seq", None, "chan")),
        check_vma=False,
    )
```

```python
import functools
import math

import jax
import jax.numpy as jnp
from jax import lax
from jax.experimental import pallas as pl
from jax.experimental.pallas import tpu as pltpu
from jax.sharding import PartitionSpec as P

D = 8192
GW = 16
MODES = 16
MED = 128
NB = 8
SLOTS = 16
LANES = 128
F32 = jnp.float32
BF16 = jnp.bfloat16
MESH = pl.DeviceIdType.MESH


def iota(shape, axis):
    return lax.broadcasted_iota(jnp.int32, shape, axis)


def split(x, parts):
    out = []
    for _ in range(parts):
        piece = x.astype(BF16)
        out.append(piece)
        x = x - piece.astype(F32)
    return out


def one_minus_exp_neg(x):
    small = x * (1.0 - x * (1 / 2) * (1.0 - x * (1 / 3) * (1.0 - x * (1 / 4) * (
        1.0 - x * (1 / 5) * (1.0 - x * (1 / 6) * (1.0 - x * (1 / 7)))))))
    return jnp.where(x < 0.1, small, 1.0 - jnp.exp(-x))


LOG2E = 1.4426950408889634
LN2 = 0.6931471805599453


def dot(a, b):
    return jnp.dot(a, b, preferred_element_type=F32)


def swap_blocks(x):
    n = x.shape[0]
    sub = iota((n, 8, LANES), 1)
    blk = iota((n, 8, LANES), 2) // GW
    gap = (blk - sub + 8) % 8
    out = x
    for d in range(1, 8):
        moved = pltpu.roll(pltpu.roll(x, 8 - d, 1), GW * d, 2)
        out = jnp.where(gap == d, moved, out)
    return out


def kernel(cfg, q_hbm, k_hbm, v_hbm, res_hbm, lam_hbm, taps_hbm, plan_hbm,
           local, hand_ref, energy_ref,
           kbuf, vbuf, qbuf, xbuf, hbuf, lam_v, res_v, taps_v, plan_v, lamc, eb, lame, gh, gt, tmat, smat, rhs, st,
           a1s, a1r, pre, a2s, a2r, a3s, a3r, items, pk, row, tin, es, er,
           in_sem, s1, r1, s2, r2, s3, r3, sx, rx, sh, rh, sp, rp, sf, rf):
    ny, nz, nc, tiles, tokens = cfg
    groups = tiles * 8
    chunks = tokens // MED
    me = lax.axis_index("seq")
    ch = lax.axis_index("chan")
    y = me // nz
    z = me % nz
    last = ny * nz - 1

    def fetch(src, dst, a, b):
        return pltpu.make_async_copy(src, dst, in_sem.at[a, b])

    def fetch_rows(c):
        rows = pl.ds(c * MED, MED)
        return (fetch(k_hbm.at[rows], kbuf.at[rows], 0, c), fetch(v_hbm.at[rows], vbuf.at[rows], 1, c))

    get_lam = fetch(lam_hbm, lam_v, 2, 0)
    get_res = fetch(res_hbm, res_v, 2, 1)
    get_taps = fetch(taps_hbm, taps_v, 2, 2)
    get_plan = fetch(plan_hbm, plan_v, 3, 0)
    get_q = fetch(q_hbm, qbuf, 3, 1)
    get_lam.start()
    for c in range(chunks):
        for copy in fetch_rows(c):
            copy.start()
    get_res.start()
    get_taps.start()
    get_plan.start()
    get_q.start()

    barrier = pltpu.get_barrier_semaphore()

    def greet(seq, chan):
        pl.semaphore_signal(barrier, inc=1, device_id=(seq, chan), device_id_type=MESH)

    for d in range(1, nz):
        greet(y * nz + (z + d) % nz, ch)
    for d in range(1, ny):
        greet(((y + d) % ny) * nz + z, ch)
    for d in range(1, nc):
        greet(me, (ch + d) % nc)
    wraps_on = (z == nz - 1) & (y < ny - 1)
    wraps_in = (z == 0) & (y > 0)

    @pl.when(wraps_on)
    def _():
        greet(me + 1, ch)

    @pl.when(wraps_in)
    def _():
        greet(me - 1, ch)

    get_lam.wait()
    lam_t = lam_v[...]
    lam2 = lam_t * LOG2E
    own16 = iota((MODES, LANES), 1) // GW
    lane128 = iota((LANES, LANES), 1)
    back = (iota((MODES, LANES), 1) - LANES).astype(F32)
    for g in range(tiles):
        spread = jnp.zeros((MODES, LANES), F32)
        for k in range(8):
            f = g * 8 + k
            col = jnp.broadcast_to(lam2[:, f:f + 1], (MODES, LANES))
            spread = jnp.where(own16 == k, col, spread)
            lamc[f * MODES:(f + 1) * MODES, :] = col
            hi, lo = split(jnp.exp2(col * back), 2)
            eb[g, k * MODES:(k + 1) * MODES, 0:LANES] = hi
            eb[g, k * MODES:(k + 1) * MODES, LANES:2 * LANES] = lo
        lame[:, g * LANES:(g + 1) * LANES] = spread

    for c in range(chunks):
        rows = pl.ds(c * MED, MED)
        for copy in fetch_rows(c):
            copy.wait()
        xbuf[rows, :] = kbuf[rows, :] * vbuf[rows, :]

    for g in range(tiles):
        lanes = slice(g * LANES, (g + 1) * LANES)
        total = None
        d128 = jnp.exp2(lame[:, lanes] * (-float(MED)))
        both = jnp.concatenate([xbuf[c * MED:(c + 1) * MED, lanes] for c in range(chunks)], axis=1)
        raw = dot(eb[g], jnp.concatenate([both, both], axis=0))
        for c in range(chunks):
            part = jnp.zeros((MODES, LANES), F32)
            for k in range(8):
                piece = raw[k * MODES:(k + 1) * MODES, c * LANES:(c + 1) * LANES]
                part = jnp.where(own16 == k, piece, part)
            total = part if total is None else total * d128 + part
            if c < chunks - 1:
                st[c, :, lanes] = total
        a1s[g] = total.astype(BF16)

    extra = wraps_on.astype(jnp.int32) + wraps_in.astype(jnp.int32)
    pl.semaphore_wait(barrier, (nz - 1) + (ny - 1) + (nc - 1) + extra)

    def remote(src, dst, send, recv, seq, chan):
        return pltpu.make_async_remote_copy(
            src_ref=src, dst_ref=dst, send_sem=send, recv_sem=recv,
            device_id=(seq, chan), device_id_type=MESH)

    def order(n):
        return sorted(range(1, n), key=lambda d: -min(d, n - d))

    sent1 = []
    for d in order(nz):
        to = (z + d) % nz
        copy = remote(a1s.at[to], a1r.at[z], s1.at[d], r1.at[z], y * nz + to, ch)
        copy.start()
        sent1.append(copy)
    a1r[z] = a1s[z]

    def halo():
        return remote(xbuf.at[pl.ds(tokens - MED, MED)], hbuf, sh, rh, me + 1, ch)

    @pl.when(me < last)
    def _():
        halo().start()

    get_plan.wait()
    plan = jnp.transpose(plan_v[...].astype(F32))
    tri = (iota((groups, groups), 1) < iota((groups, groups), 0)).astype(BF16)

    @pl.when(me == last)
    def _():
        who = iota((groups, LANES), 1).astype(F32)
        hits = jnp.zeros((groups, LANES), F32)
        for b in range(NB + 1):
            hits = hits + (plan[:, b:b + 1] == who).astype(F32)
        before = dot(tri, hits.astype(BF16))
        slots = jnp.full((groups, LANES), -1.0, F32)
        for b in range(NB):
            reader = plan[:, b:b + 1]
            rank = jnp.sum(jnp.where(reader == who, before, 0.0), axis=1, keepdims=True)
            slots = jnp.where(who == b, reader * SLOTS + rank, slots)
        slots_t = jnp.transpose(slots)
        for b in range(NB):
            for half in range(2):
                for g in range(tiles):
                    tile = xbuf[tokens - MED + b * MODES:tokens - MED + (b + 1) * MODES,
                                g * LANES:(g + 1) * LANES].astype(F32)[half * 8:half * 8 + 8]
                    items[b * groups + g * 8:b * groups + g * 8 + 8,
                          half * LANES:(half + 1) * LANES] = swap_blocks(tile[None])[0]
        for part in range(ny):
            count = nz * SLOTS
            base = part * count
            acc = jnp.zeros((count, 2 * LANES), F32)
            target = (iota((count, groups), 0) + base).astype(F32)
            for b in range(NB):
                pick = (target == slots_t[b:b + 1, 0:groups]).astype(BF16)
                acc = acc + dot(pick, items[b * groups:(b + 1) * groups, :].astype(BF16))
            packed = acc.astype(BF16).reshape(nz, SLOTS, 2 * LANES)
            if part == ny - 1:
                row[...] = packed
            else:
                pk[part] = packed

    def pack_copy(part):
        return remote(pk.at[part], row, sp.at[part], rp, part * nz + nz - 1, ch)

    @pl.when(me == last)
    def _():
        for part in range(ny - 1):
            pack_copy(part).start()

    get_res.wait()
    get_taps.wait()
    weight_t = res_v[...] * jnp.sqrt(one_minus_exp_neg(2.0 * lam_t))
    perm = (iota((LANES, LANES), 0) == (LANES - lane128) % LANES).astype(BF16)
    flipped = dot(jnp.concatenate(split(taps_v[...], 3), axis=0), perm)
    flipped = flipped[0:groups] + flipped[groups:2 * groups] + flipped[2 * groups:3 * groups]
    gt[...] = flipped
    zero16 = iota((MODES, LANES), 1) == 0
    for g in range(tiles):
        sums = []
        for k in range(8):
            f = g * 8 + k
            at = slice(k * MODES, (k + 1) * MODES)
            w = jnp.broadcast_to(weight_t[:, f:f + 1], (MODES, LANES))
            e = eb[g, at, 0:LANES].astype(F32) + eb[g, at, LANES:2 * LANES].astype(F32)
            sums.append(jnp.sum(jnp.where(zero16, w, w * e), axis=0, keepdims=True))
        gh[g * 8:(g + 1) * 8, :] = jnp.concatenate(sums, axis=0) + flipped[g * 8:(g + 1) * 8]

    def conv_tile(g, carry):
        lanes = pl.ds(pl.multiple_of(g * LANES, LANES), LANES)
        rows8 = pl.ds(pl.multiple_of(g * 8, 8), 8)
        full = gh[rows8, :]
        taps = gt[rows8, :]
        lower = iota((LANES, LANES), 1) <= iota((LANES, LANES), 0)
        which = iota((MED, LANES), 1) // GW
        x0 = xbuf[0:MED, lanes]
        x1 = xbuf[MED:2 * MED, lanes]
        x2 = xbuf[2 * MED:3 * MED, lanes]
        for k in range(8):
            a = pltpu.roll(jnp.broadcast_to(full[k:k + 1], (LANES, LANES)), 0, 1, stride=1, stride_axis=0)
            b = pltpu.roll(jnp.broadcast_to(taps[k:k + 1], (LANES, LANES)), 0, 1, stride=1, stride_axis=0)
            cols = slice(k * LANES, (k + 1) * LANES)
            hi, lo = split(jnp.where(lower, a, 0.0), 2)
            tmat[g, 0:LANES, cols] = hi
            tmat[g, 2 * LANES:3 * LANES, cols] = lo
            hi, lo = split(jnp.where(lower, 0.0, b), 2)
            tmat[g, LANES:2 * LANES, cols] = hi
            tmat[g, 3 * LANES:4 * LANES, cols] = lo
            keep = (which == k).astype(BF16)
            rhs[cols, 0:LANES] = x0 * keep
            rhs[cols, LANES:2 * LANES] = x1 * keep
            rhs[cols, 2 * LANES:3 * LANES] = x2 * keep
        out = dot(tmat[g, 0:2 * LANES, :], rhs[:, 0:2 * LANES])
        out = out + dot(tmat[g, 2 * LANES:4 * LANES, :], rhs[:, 0:2 * LANES])
        out2 = dot(tmat[g, 0:LANES, :], rhs[:, 2 * LANES:3 * LANES])
        out2 = out2 + dot(tmat[g, 2 * LANES:3 * LANES, :], rhs[:, 2 * LANES:3 * LANES])
        local[0:MED, lanes] = out[0:LANES, 0:LANES]
        local[MED:2 * MED, lanes] = out[0:LANES, LANES:2 * LANES] + out[LANES:2 * LANES, 0:LANES]
        local[2 * MED:3 * MED, lanes] = out2 + out[LANES:2 * LANES, LANES:2 * LANES]
        return carry

    early = 3 * tiles // 8
    lax.fori_loop(0, early, conv_tile, 0)

    mine = pl.ds(pl.multiple_of(z * LANES, LANES), LANES)
    lam_s = lame[:, mine]
    d_dev = jnp.exp2(lam_s * (-float(tokens)))
    for d in range(1, nz):
        frm = (z - d + nz) % nz
        remote(a1s.at[0], a1r.at[frm], s1.at[d], r1.at[frm], me, ch).wait_recv()
    run = jnp.zeros((MODES, LANES), F32)
    for i in range(nz):
        pre[i] = run
        run = run * d_dev + a1r[i].astype(F32)
    a2s[...] = run.astype(BF16)

    sent2 = []
    for d in order(ny):
        to = (y + d) % ny
        copy = remote(a2s, a2r.at[y], s2.at[d], r2.at[y], to * nz + z, ch)
        copy.start()
        sent2.append(copy)
    a2r[y] = a2s[...]

    lax.fori_loop(early, tiles, conv_tile, 0)

    for g in range(tiles):
        lanes = slice(g * LANES, (g + 1) * LANES)
        rates = lamc[lanes, :]
        weight = jnp.concatenate(
            [jnp.broadcast_to(weight_t[:, f:f + 1], (MODES, LANES)) for f in range(g * 8, g * 8 + 8)], axis=0)
        at = lane128.astype(F32)
        for c in range(chunks):
            s = weight * jnp.exp2(-rates * (at + float(c * MED)))
            smat[c * MED:(c + 1) * MED, lanes] = jnp.transpose(s).astype(BF16)
        same = (iota((LANES, LANES), 0) // MODES) == (iota((LANES, LANES), 1) // GW)
        pieces = []
        for c in range(chunks - 1):
            state = jnp.concatenate([st[c, :, lanes]] * 8, axis=0)
            pieces.append(jnp.where(same, state, 0.0))
        hi, lo = split(jnp.concatenate(pieces, axis=1), 2)
        factor = smat[0:MED, lanes]
        out = dot(jnp.concatenate([factor, factor], axis=1), jnp.concatenate([hi, lo], axis=0))
        for c in range(chunks - 1):
            rows = slice((c + 1) * MED, (c + 2) * MED)
            local[rows, lanes] = local[rows, lanes] + out[:, c * LANES:(c + 1) * LANES]

    d_row = jnp.exp2(lam_s * (-float(tokens * nz)))
    for d in range(1, ny):
        frm = (y - d + ny) % ny
        remote(a2s, a2r.at[frm], s2.at[d], r2.at[frm], me, ch).wait_recv()
    run = jnp.zeros((MODES, LANES), F32)
    above = jnp.zeros((MODES, LANES), F32)
    for i in range(ny):
        above = jnp.where(y == i, run, above)
        run = run * d_row + a2r[i].astype(F32)
    norm_s = jnp.sqrt(one_minus_exp_neg(lam_s * (2.0 * LN2)))
    final = (run * norm_s).astype(BF16)
    for i in range(nz):
        a3s[i, 0] = (above + pre[i]).astype(BF16)
        a3s[i, 1] = final
        above = above * d_dev

    sent3 = []
    for d in order(nz):
        to = (z + d) % nz
        copy = remote(a3s.at[to], a3r.at[z], s3.at[d], r3.at[z], y * nz + to, ch)
        copy.start()
        sent3.append(copy)
    a3r[z] = a3s[z]

    def hop_copy(to):
        return remote(row.at[to], tin, sf.at[to], rf, y * nz + to, ch)

    @pl.when((z == nz - 1) & (me != last))
    def _():
        remote(pk.at[0], row, sp.at[0], rp, me, ch).wait_recv()

    @pl.when(z == nz - 1)
    def _():
        for to in range(nz - 1):
            hop_copy(to).start()
        tin[...] = row[nz - 1]

    @pl.when(me > 0)
    def _():
        remote(xbuf.at[pl.ds(tokens - MED, MED)], hbuf, sh, rh, me, ch).wait_recv()

        def halo_tile(g, carry):
            lanes = pl.ds(pl.multiple_of(g * LANES, LANES), LANES)
            which = iota((MED, LANES), 1) // GW
            xh = hbuf[:, lanes]
            for k in range(8):
                rhs[k * LANES:(k + 1) * LANES, 0:LANES] = xh * (which == k).astype(BF16)
            out = dot(tmat[g, LANES:2 * LANES, :], rhs[:, 0:LANES])
            out = out + dot(tmat[g, 3 * LANES:4 * LANES, :], rhs[:, 0:LANES])
            local[0:MED, lanes] = local[0:MED, lanes] + out
            return carry

        lax.fori_loop(0, tiles, halo_tile, 0)

    get_q.wait()
    for d in range(1, nz):
        frm = (z - d + nz) % nz
        remote(a3s.at[0], a3r.at[frm], s3.at[d], r3.at[frm], me, ch).wait_recv()

    power = jnp.zeros((tokens, LANES), F32)
    wide = 2 * LANES
    same2 = ((iota((wide, wide), 0) // MODES) == (iota((wide, wide), 1) // GW)).astype(BF16)
    for g in range(tiles // 2):
        lanes = slice(g * wide, (g + 1) * wide)
        state = jnp.concatenate([a3r[2 * g, 0], a3r[2 * g + 1, 0]], axis=1)
        spread = jnp.concatenate([state] * 16, axis=0) * same2
        cross = dot(smat[:, lanes], spread)
        gated = qbuf[:, lanes].astype(F32) * (local[:, lanes] + cross)
        local[:, lanes] = gated
        sq = gated * gated
        power = power + sq[:, 0:LANES] + sq[:, LANES:wide]
    es[...] = jnp.sum(jnp.transpose(power), axis=0, keepdims=True)

    sentx = []
    for d in order(nc):
        to = (ch + d) % nc
        copy = remote(es, er.at[ch], sx.at[d], rx.at[ch], me, to)
        copy.start()
        sentx.append(copy)
    er[ch] = es[...]

    mine_hit = (plan == me.astype(F32)).astype(F32)
    hit = jnp.sum(mine_hit, axis=1, keepdims=True)
    before = dot(tri, jnp.broadcast_to(hit, (groups, 2 * LANES)).astype(BF16))
    slot = (iota((groups, 2 * LANES), 1) // GW).astype(F32)
    wants = jnp.where(before == slot, mine_hit[:, NB:NB + 1], 0.0).astype(BF16)
    picked = jnp.zeros((MODES, 2 * LANES), F32)
    delta = ((iota((LANES, 2 * LANES), 0) % GW) == (iota((LANES, 2 * LANES), 1) % GW)).astype(F32)
    for g in range(tiles):
        rep = ((iota((LANES, groups), 0) // GW + g * 8) == iota((LANES, groups), 1)).astype(BF16)
        choose = (dot(rep, wants) * delta).astype(BF16)
        picked = picked + dot(a3r[g, 1], choose)

    @pl.when(z != nz - 1)
    def _():
        remote(row.at[0], tin, sf.at[0], rf, me, ch).wait_recv()

    tails = tin[...].astype(F32)
    for a in range(2):
        for b in range(2):
            block = swap_blocks(tails[8 * a:8 * a + 8, b * LANES:(b + 1) * LANES][None])[0]
            block = block + picked[8 * b:8 * b + 8, a * LANES:(a + 1) * LANES]
            for k in range(8):
                j = a * 8 + k
                if j < 10:
                    hand_ref[j, 8 * b:8 * b + 8, :] = block[:, k * GW:(k + 1) * GW]

    for copy in sent1 + sent2 + sent3:
        copy.wait_send()

    @pl.when(me < last)
    def _():
        halo().wait_send()

    @pl.when(me == last)
    def _():
        for part in range(ny - 1):
            pack_copy(part).wait_send()

    @pl.when(z == nz - 1)
    def _():
        for to in range(nz - 1):
            hop_copy(to).wait_send()

    for d in range(1, nc):
        frm = (ch - d + nc) % nc
        remote(es, er.at[frm], sx.at[d], rx.at[frm], me, ch).wait_recv()
    energy = er[0]
    for i in range(1, nc):
        energy = energy + er[i]
    energy_ref[...] = energy
    for copy in sentx:
        copy.wait_send()


def finish(width, gated_ref, hand_ref, energy_ref, gain_ref, out_hbm, hand_hbm, obuf, sem):
    tokens, channels = gated_ref.shape
    chunks = tokens // MED
    give = pltpu.make_async_copy(hand_ref, hand_hbm, sem.at[chunks])
    give.start()
    scale = lax.rsqrt(energy_ref[...] / width + 1e-05)
    scale = jnp.transpose(jnp.broadcast_to(scale, (LANES, tokens)))
    copies = []
    for c in range(chunks):
        rows = slice(c * MED, (c + 1) * MED)
        for g in range(channels // LANES):
            lanes = slice(g * LANES, (g + 1) * LANES)
            obuf[rows, lanes] = (gated_ref[rows, lanes] * scale[rows] * gain_ref[:, lanes]).astype(BF16)
        copy = pltpu.make_async_copy(obuf.at[pl.ds(c * MED, MED)], out_hbm.at[pl.ds(c * MED, MED)], sem.at[c])
        copy.start()
        copies.append(copy)
    for copy in copies:
        copy.wait()
    give.wait()


def per_device(query_rows, key_rows, value_rows, residues, decay_rates, medium_taps, out_gain, reader_plan):
    tokens, channels = query_rows.shape
    tiles = channels // LANES
    groups = tiles * 8
    seq = lax.axis_size("seq")
    nz = math.isqrt(seq)
    ny = seq // nz
    nc = lax.axis_size("chan")
    cfg = (ny, nz, nc, tiles, tokens)
    chunks = tokens // MED
    vm = pltpu.VMEM
    dma = pltpu.SemaphoreType.DMA
    scratch = [
        vm((tokens, channels), BF16), vm((tokens, channels), BF16), vm((tokens, channels), BF16),
        vm((tokens, channels), BF16), vm((MED, channels), BF16),
        vm((MODES, groups), F32), vm((MODES, groups), F32), vm((groups, MED), F32), vm((NB + 1, groups), jnp.int32),
        vm((channels, LANES), F32), vm((tiles, LANES, 2 * LANES), BF16),
        vm((MODES, channels), F32), vm((groups, LANES), F32), vm((groups, LANES), F32),
        vm((tiles, 4 * LANES, 8 * LANES), BF16), vm((tokens, channels), BF16),
        vm((8 * LANES, 3 * LANES), BF16),
        vm((chunks, MODES, channels), F32),
        vm((nz, MODES, LANES), BF16), vm((nz, MODES, LANES), BF16), vm((nz, MODES, LANES), F32),
        vm((MODES, LANES), BF16), vm((ny, MODES, LANES), BF16),
        vm((nz, 2, MODES, LANES), BF16), vm((nz, 2, MODES, LANES), BF16),
        vm((NB * groups, 2 * LANES), F32), vm((ny - 1, nz, SLOTS, 2 * LANES), BF16),
        vm((nz, SLOTS, 2 * LANES), BF16), vm((SLOTS, 2 * LANES), BF16),
        vm((1, tokens), F32), vm((nc, 1, tokens), F32),
        dma((4, chunks)),
        dma((nz,)), dma((nz,)), dma((ny,)), dma((ny,)), dma((nz,)), dma((nz,)), dma((nc,)), dma((nc,)),
        dma, dma, dma((ny,)), dma, dma((nz,)), dma,
    ]
    hbm = pl.BlockSpec(memory_space=pltpu.HBM)
    vmem = pl.BlockSpec(memory_space=pltpu.VMEM)
    gated, hand, energy = pl.pallas_call(
        functools.partial(kernel, cfg),
        name="hyena",
        out_shape=(
            jax.ShapeDtypeStruct((tokens, channels), F32),
            jax.ShapeDtypeStruct((10, MODES, GW), F32),
            jax.ShapeDtypeStruct((1, tokens), F32),
        ),
        in_specs=[hbm] * 7,
        out_specs=(vmem, vmem, vmem),
        scratch_shapes=scratch,
        compiler_params=pltpu.CompilerParams(
            collective_id=0, has_side_effects=True, vmem_limit_bytes=48 * 1024 * 1024),
    )(*[pltpu.with_memory_space_constraint(a, pltpu.HBM) for a in (query_rows, key_rows, value_rows, residues.T, decay_rates.T, medium_taps, reader_plan.T)])
    return pl.pallas_call(
        functools.partial(finish, nc * channels),
        name="finish",
        out_shape=(
            jax.ShapeDtypeStruct((tokens, channels), BF16),
            jax.ShapeDtypeStruct((10, MODES, GW), F32),
        ),
        in_specs=[vmem] * 4,
        out_specs=(hbm, hbm),
        scratch_shapes=[vm((tokens, channels), BF16), dma((chunks + 1,))],
        compiler_params=pltpu.CompilerParams(vmem_limit_bytes=48 * 1024 * 1024),
    )(gated, hand, energy, out_gain.reshape(1, channels))


def solution(mesh):
    placed = (
        P("seq", "chan"),
        P("seq", "chan"),
        P("seq", "chan"),
        P("chan", None),
        P("chan", None),
        P("chan", None),
        P("chan"),
        P("chan", None),
    )
    return jax.shard_map(
        per_device,
        mesh=mesh,
        in_specs=placed,
        out_specs=(P("seq", "chan"), P("seq", None, "chan")),
        check_vma=False,
    )
```

```python
import functools
import math

import jax
import jax.numpy as jnp
from jax import lax
from jax.experimental import pallas as pl
from jax.experimental.pallas import tpu as pltpu
from jax.sharding import PartitionSpec as P

D = 8192
GW = 16
MODES = 16
MED = 128
NB = 8
SLOTS = 16
LANES = 128
F32 = jnp.float32
BF16 = jnp.bfloat16
MESH = pl.DeviceIdType.MESH


def iota(shape, axis):
    return lax.broadcasted_iota(jnp.int32, shape, axis)


def split(x, parts):
    out = []
    for _ in range(parts):
        piece = x.astype(BF16)
        out.append(piece)
        x = x - piece.astype(F32)
    return out


def one_minus_exp_neg(x):
    small = x * (1.0 - x * (1 / 2) * (1.0 - x * (1 / 3) * (1.0 - x * (1 / 4) * (
        1.0 - x * (1 / 5) * (1.0 - x * (1 / 6) * (1.0 - x * (1 / 7)))))))
    return jnp.where(x < 0.1, small, 1.0 - jnp.exp(-x))


LOG2E = 1.4426950408889634
LN2 = 0.6931471805599453


def dot(a, b):
    return jnp.dot(a, b, preferred_element_type=F32)


def swap_blocks(x):
    n = x.shape[0]
    sub = iota((n, 8, LANES), 1)
    blk = iota((n, 8, LANES), 2) // GW
    gap = (blk - sub + 8) % 8
    out = x
    for d in range(1, 8):
        moved = pltpu.roll(pltpu.roll(x, 8 - d, 1), GW * d, 2)
        out = jnp.where(gap == d, moved, out)
    return out


def kernel(cfg, q_hbm, k_hbm, v_hbm, res_hbm, lam_hbm, taps_hbm, plan_hbm,
           local, hand_ref, energy_ref,
           kbuf, vbuf, qbuf, xbuf, hbuf, lam_v, res_v, taps_v, plan_v, lamc, eb, lame, gh, gt, tmat, smat, rhs, st,
           a1s, a1r, pre, a2s, a2r, a3s, a3r, items, pk, row, tin, es, er,
           in_sem, s1, r1, s2, r2, s3, r3, sx, rx, sh, rh, sp, rp, sf, rf):
    ny, nz, nc, tiles, tokens = cfg
    groups = tiles * 8
    chunks = tokens // MED
    me = lax.axis_index("seq")
    ch = lax.axis_index("chan")
    y = me // nz
    z = me % nz
    last = ny * nz - 1

    def fetch(src, dst, a, b):
        return pltpu.make_async_copy(src, dst, in_sem.at[a, b])

    def fetch_rows(c):
        rows = pl.ds(c * MED, MED)
        return (fetch(k_hbm.at[rows], kbuf.at[rows], 0, c), fetch(v_hbm.at[rows], vbuf.at[rows], 1, c))

    get_lam = fetch(lam_hbm, lam_v, 2, 0)
    get_res = fetch(res_hbm, res_v, 2, 1)
    get_taps = fetch(taps_hbm, taps_v, 2, 2)
    get_plan = fetch(plan_hbm, plan_v, 3, 0)
    get_q = fetch(q_hbm, qbuf, 3, 1)
    get_lam.start()
    for c in range(chunks):
        for copy in fetch_rows(c):
            copy.start()
    get_res.start()
    get_taps.start()
    get_plan.start()
    get_q.start()

    barrier = pltpu.get_barrier_semaphore()

    def greet(seq, chan):
        pl.semaphore_signal(barrier, inc=1, device_id=(seq, chan), device_id_type=MESH)

    for d in range(1, nz):
        greet(y * nz + (z + d) % nz, ch)
    for d in range(1, ny):
        greet(((y + d) % ny) * nz + z, ch)
    for d in range(1, nc):
        greet(me, (ch + d) % nc)
    wraps_on = (z == nz - 1) & (y < ny - 1)
    wraps_in = (z == 0) & (y > 0)

    @pl.when(wraps_on)
    def _():
        greet(me + 1, ch)

    @pl.when(wraps_in)
    def _():
        greet(me - 1, ch)

    get_lam.wait()
    lam_t = lam_v[...]
    lam2 = lam_t * LOG2E
    own16 = iota((MODES, LANES), 1) // GW
    lane128 = iota((LANES, LANES), 1)
    back = (iota((MODES, LANES), 1) - LANES).astype(F32)
    for g in range(tiles):
        spread = jnp.zeros((MODES, LANES), F32)
        for k in range(8):
            f = g * 8 + k
            col = jnp.broadcast_to(lam2[:, f:f + 1], (MODES, LANES))
            spread = jnp.where(own16 == k, col, spread)
            lamc[f * MODES:(f + 1) * MODES, :] = col
            eb[g, k * MODES:(k + 1) * MODES, :] = jnp.exp2(col * back).astype(BF16)
        lame[:, g * LANES:(g + 1) * LANES] = spread

    for c in range(chunks):
        rows = pl.ds(c * MED, MED)
        for copy in fetch_rows(c):
            copy.wait()
        xbuf[rows, :] = kbuf[rows, :] * vbuf[rows, :]

    for g in range(tiles):
        lanes = slice(g * LANES, (g + 1) * LANES)
        total = None
        d128 = jnp.exp2(lame[:, lanes] * (-float(MED)))
        both = jnp.concatenate([xbuf[c * MED:(c + 1) * MED, lanes] for c in range(chunks)], axis=1)
        raw = dot(eb[g], both)
        for c in range(chunks):
            part = jnp.zeros((MODES, LANES), F32)
            for k in range(8):
                piece = raw[k * MODES:(k + 1) * MODES, c * LANES:(c + 1) * LANES]
                part = jnp.where(own16 == k, piece, part)
            total = part if total is None else total * d128 + part
            if c < chunks - 1:
                st[c, :, lanes] = total
        a1s[g] = total.astype(BF16)

    extra = wraps_on.astype(jnp.int32) + wraps_in.astype(jnp.int32)
    pl.semaphore_wait(barrier, (nz - 1) + (ny - 1) + (nc - 1) + extra)

    def remote(src, dst, send, recv, seq, chan):
        return pltpu.make_async_remote_copy(
            src_ref=src, dst_ref=dst, send_sem=send, recv_sem=recv,
            device_id=(seq, chan), device_id_type=MESH)

    def settle(ref, sem):
        pltpu.make_async_copy(ref, ref, sem).wait()

    def order(n):
        return sorted(range(1, n), key=lambda d: -min(d, n - d))

    for d in order(nz):
        to = (z + d) % nz
        copy = remote(a1s.at[to], a1r.at[z], s1, r1, y * nz + to, ch)
        copy.start()
    a1r[z] = a1s[z]

    def halo():
        return remote(xbuf.at[pl.ds(tokens - MED, MED)], hbuf, sh, rh, me + 1, ch)

    get_plan.wait()
    plan = jnp.transpose(plan_v[...].astype(F32))
    tri = (iota((groups, groups), 1) < iota((groups, groups), 0)).astype(BF16)

    @pl.when(me == last)
    def _():
        who = iota((groups, LANES), 1).astype(F32)
        hits = jnp.zeros((groups, LANES), F32)
        for b in range(NB + 1):
            hits = hits + (plan[:, b:b + 1] == who).astype(F32)
        before = dot(tri, hits.astype(BF16))
        slots = jnp.full((groups, LANES), -1.0, F32)
        for b in range(NB):
            reader = plan[:, b:b + 1]
            rank = jnp.sum(jnp.where(reader == who, before, 0.0), axis=1, keepdims=True)
            down = jnp.floor((reader + 0.5) * (1.0 / nz))
            place = (reader - down * nz) * ny + down
            slots = jnp.where(who == b, place * SLOTS + rank, slots)
        slots_t = jnp.transpose(slots)
        for b in range(NB):
            for half in range(2):
                for g in range(tiles):
                    tile = xbuf[tokens - MED + b * MODES:tokens - MED + (b + 1) * MODES,
                                g * LANES:(g + 1) * LANES].astype(F32)[half * 8:half * 8 + 8]
                    items[b * groups + g * 8:b * groups + g * 8 + 8,
                          half * LANES:(half + 1) * LANES] = swap_blocks(tile[None])[0]
        wanted = [jnp.concatenate([slots_t[b:b + 1, 0:groups] for b in range(4 * i, 4 * i + 4)], axis=1)
                  for i in range(NB // 4)]
        for part in range(nz):
            count = ny * SLOTS
            base = part * count
            acc = jnp.zeros((count, 2 * LANES), F32)
            target = (iota((count, 4 * groups), 0) + base).astype(F32)
            for b in range(NB // 4):
                pick = (target == wanted[b]).astype(BF16)
                acc = acc + dot(pick, items[4 * b * groups:4 * (b + 1) * groups, :].astype(BF16))
            packed = acc.astype(BF16).reshape(ny, SLOTS, 2 * LANES)
            if part == nz - 1:
                row[...] = packed
            else:
                pk[part] = packed

    def pack_copy(part):
        return remote(pk.at[part], row, sp, rp, (ny - 1) * nz + part, ch)

    @pl.when(me == last)
    def _():
        for part in range(nz - 1):
            pack_copy(part).start()

    get_res.wait()
    get_taps.wait()
    weight_t = res_v[...] * jnp.sqrt(one_minus_exp_neg(2.0 * lam_t))
    perm = (iota((LANES, LANES), 0) == (LANES - lane128) % LANES).astype(BF16)
    flipped = dot(jnp.concatenate(split(taps_v[...], 3), axis=0), perm)
    flipped = flipped[0:groups] + flipped[groups:2 * groups] + flipped[2 * groups:3 * groups]
    gt[...] = flipped
    zero16 = iota((MODES, LANES), 1) == 0
    for g in range(tiles):
        sums = []
        for k in range(8):
            f = g * 8 + k
            w = jnp.broadcast_to(weight_t[:, f:f + 1], (MODES, LANES))
            e = jnp.exp2(lamc[f * MODES:(f + 1) * MODES, :] * back)
            sums.append(jnp.sum(jnp.where(zero16, w, w * e), axis=0, keepdims=True))
        gh[g * 8:(g + 1) * 8, :] = jnp.concatenate(sums, axis=0) + flipped[g * 8:(g + 1) * 8]

    def conv_build(g, side):
        lanes = pl.ds(pl.multiple_of(g * LANES, LANES), LANES)
        rows8 = pl.ds(pl.multiple_of(g * 8, 8), 8)
        full = gh[rows8, :]
        taps = gt[rows8, :]
        lower = iota((LANES, LANES), 1) <= iota((LANES, LANES), 0)
        which = iota((MED, LANES), 1) // GW
        x0 = xbuf[0:MED, lanes]
        x1 = xbuf[MED:2 * MED, lanes]
        x2 = xbuf[2 * MED:3 * MED, lanes]
        for k in range(8):
            a = pltpu.roll(jnp.broadcast_to(full[k:k + 1], (LANES, LANES)), 0, 1, stride=1, stride_axis=0)
            b = pltpu.roll(jnp.broadcast_to(taps[k:k + 1], (LANES, LANES)), 0, 1, stride=1, stride_axis=0)
            cols = slice(k * LANES, (k + 1) * LANES)
            tmat[g, 0:LANES, cols] = jnp.where(lower, a, 0.0).astype(BF16)
            tmat[g, LANES:2 * LANES, cols] = jnp.where(lower, 0.0, b).astype(BF16)
            keep = (which == k).astype(BF16)
            rhs[side, cols, 0:LANES] = x0 * keep
            rhs[side, cols, LANES:2 * LANES] = x1 * keep
            rhs[side, cols, 2 * LANES:3 * LANES] = x2 * keep

    def conv_apply(g, side):
        lanes = pl.ds(pl.multiple_of(g * LANES, LANES), LANES)
        out = dot(tmat[g], rhs[side, :, 0:2 * LANES])
        out2 = dot(tmat[g, 0:LANES, :], rhs[side, :, 2 * LANES:3 * LANES])
        local[0:MED, lanes] = out[0:LANES, 0:LANES]
        local[MED:2 * MED, lanes] = out[0:LANES, LANES:2 * LANES] + out[LANES:2 * LANES, 0:LANES]
        local[2 * MED:3 * MED, lanes] = out2 + out[LANES:2 * LANES, LANES:2 * LANES]

    def conv_pair(p, carry):
        conv_build(2 * p, 0)
        conv_build(2 * p + 1, 1)
        conv_apply(2 * p, 0)
        conv_apply(2 * p + 1, 1)
        return carry

    pairs = tiles // 2
    early = jnp.where(me == last, pairs // 4, 3 * pairs // 4)
    lax.fori_loop(0, early, conv_pair, 0)

    mine = pl.ds(pl.multiple_of(z * LANES, LANES), LANES)
    lam_s = lame[:, mine]
    d_dev = jnp.exp2(lam_s * (-float(tokens)))
    settle(a1r.at[pl.ds(0, nz - 1)], r1)
    run = jnp.zeros((MODES, LANES), F32)
    for i in range(nz):
        pre[i] = run
        run = run * d_dev + a1r[i].astype(F32)
    a2s[...] = run.astype(BF16)

    for d in order(ny):
        to = (y + d) % ny
        copy = remote(a2s, a2r.at[y], s2, r2, to * nz + z, ch)
        copy.start()
    a2r[y] = a2s[...]

    @pl.when(me < last)
    def _():
        halo().start()

    lax.fori_loop(early, pairs, conv_pair, 0)

    for g in range(tiles):
        lanes = slice(g * LANES, (g + 1) * LANES)
        rates = lamc[lanes, :]
        weight = jnp.concatenate(
            [jnp.broadcast_to(weight_t[:, f:f + 1], (MODES, LANES)) for f in range(g * 8, g * 8 + 8)], axis=0)
        at = lane128.astype(F32)
        for c in range(chunks):
            s = weight * jnp.exp2(-rates * (at + float(c * MED)))
            smat[c * MED:(c + 1) * MED, lanes] = jnp.transpose(s).astype(BF16)
        same = (iota((LANES, LANES), 0) // MODES) == (iota((LANES, LANES), 1) // GW)
        pieces = []
        for c in range(chunks - 1):
            state = jnp.concatenate([st[c, :, lanes]] * 8, axis=0)
            pieces.append(jnp.where(same, state, 0.0))
        hi, lo = split(jnp.concatenate(pieces, axis=1), 2)
        factor = smat[0:MED, lanes]
        out = dot(jnp.concatenate([factor, factor], axis=1), jnp.concatenate([hi, lo], axis=0))
        for c in range(chunks - 1):
            rows = slice((c + 1) * MED, (c + 2) * MED)
            local[rows, lanes] = local[rows, lanes] + out[:, c * LANES:(c + 1) * LANES]

    d_row = jnp.exp2(lam_s * (-float(tokens * nz)))
    settle(a2r.at[pl.ds(0, ny - 1)], r2)
    run = jnp.zeros((MODES, LANES), F32)
    above = jnp.zeros((MODES, LANES), F32)
    for i in range(ny):
        above = jnp.where(y == i, run, above)
        run = run * d_row + a2r[i].astype(F32)
    norm_s = jnp.sqrt(one_minus_exp_neg(lam_s * (2.0 * LN2)))
    final = (run * norm_s).astype(BF16)
    for i in range(nz):
        a3s[i, 0] = (above + pre[i]).astype(BF16)
        a3s[i, 1] = final
        above = above * d_dev

    for d in order(nz):
        to = (z + d) % nz
        copy = remote(a3s.at[to], a3r.at[z], s3, r3, y * nz + to, ch)
        copy.start()
    a3r[z] = a3s[z]

    def hop_copy(to):
        return remote(row.at[to], tin, sf, rf, to * nz + z, ch)

    @pl.when((y == ny - 1) & (me != last))
    def _():
        remote(pk.at[0], row, sp, rp, me, ch).wait_recv()

    @pl.when(y == ny - 1)
    def _():
        for to in range(ny - 1):
            hop_copy(to).start()
        tin[...] = row[ny - 1]

    @pl.when(me > 0)
    def _():
        remote(xbuf.at[pl.ds(tokens - MED, MED)], hbuf, sh, rh, me, ch).wait_recv()

        def halo_tile(g, carry):
            lanes = pl.ds(pl.multiple_of(g * LANES, LANES), LANES)
            which = iota((MED, LANES), 1) // GW
            xh = hbuf[:, lanes]
            for k in range(8):
                rhs[0, k * LANES:(k + 1) * LANES, 0:LANES] = xh * (which == k).astype(BF16)
            out = dot(tmat[g, LANES:2 * LANES, :], rhs[0, :, 0:LANES])
            local[0:MED, lanes] = local[0:MED, lanes] + out
            return carry

        lax.fori_loop(0, tiles, halo_tile, 0)

    get_q.wait()
    settle(a3r.at[pl.ds(0, nz - 1)], r3)

    power = jnp.zeros((tokens, LANES), F32)
    wide = 2 * LANES
    same2 = ((iota((wide, wide), 0) // MODES) == (iota((wide, wide), 1) // GW)).astype(BF16)
    for g in range(tiles // 2):
        lanes = slice(g * wide, (g + 1) * wide)
        state = jnp.concatenate([a3r[2 * g, 0], a3r[2 * g + 1, 0]], axis=1)
        spread = jnp.concatenate([state] * 16, axis=0) * same2
        cross = dot(smat[:, lanes], spread)
        gated = qbuf[:, lanes].astype(F32) * (local[:, lanes] + cross)
        local[:, lanes] = gated
        sq = gated * gated
        power = power + sq[:, 0:LANES] + sq[:, LANES:wide]
    es[...] = jnp.sum(jnp.transpose(power), axis=0, keepdims=True)

    for d in order(nc):
        to = (ch + d) % nc
        copy = remote(es, er.at[ch], sx, rx, me, to)
        copy.start()
    er[ch] = es[...]

    mine_hit = (plan == me.astype(F32)).astype(F32)
    hit = jnp.sum(mine_hit, axis=1, keepdims=True)
    before = dot(tri, jnp.broadcast_to(hit, (groups, 2 * LANES)).astype(BF16))
    slot = (iota((groups, 2 * LANES), 1) // GW).astype(F32)
    wants = jnp.where(before == slot, mine_hit[:, NB:NB + 1], 0.0).astype(BF16)
    picked = jnp.zeros((MODES, 2 * LANES), F32)
    delta = ((iota((LANES, 2 * LANES), 0) % GW) == (iota((LANES, 2 * LANES), 1) % GW)).astype(F32)
    for g in range(tiles):
        rep = ((iota((LANES, groups), 0) // GW + g * 8) == iota((LANES, groups), 1)).astype(BF16)
        choose = (dot(rep, wants) * delta).astype(BF16)
        picked = picked + dot(a3r[g, 1], choose)

    @pl.when(y != ny - 1)
    def _():
        remote(row.at[0], tin, sf, rf, me, ch).wait_recv()

    tails = tin[...].astype(F32)
    for a in range(2):
        for b in range(2):
            block = swap_blocks(tails[8 * a:8 * a + 8, b * LANES:(b + 1) * LANES][None])[0]
            block = block + picked[8 * b:8 * b + 8, a * LANES:(a + 1) * LANES]
            for k in range(8):
                j = a * 8 + k
                if j < 10:
                    hand_ref[j, 8 * b:8 * b + 8, :] = block[:, k * GW:(k + 1) * GW]

    settle(a1s.at[pl.ds(0, nz - 1)], s1)
    settle(a2r.at[pl.ds(0, ny - 1)], s2)
    settle(a3s.at[pl.ds(0, nz - 1)], s3)

    @pl.when(me < last)
    def _():
        halo().wait_send()

    @pl.when(me == last)
    def _():
        settle(pk, sp)

    @pl.when(y == ny - 1)
    def _():
        settle(row.at[pl.ds(0, ny - 1)], sf)

    settle(er.at[pl.ds(0, nc - 1)], rx)
    energy = er[0]
    for i in range(1, nc):
        energy = energy + er[i]
    energy_ref[...] = energy
    settle(er.at[pl.ds(0, nc - 1)], sx)


def finish(width, gated_ref, hand_ref, energy_ref, gain_ref, out_hbm, hand_hbm, obuf, sem):
    tokens, channels = gated_ref.shape
    chunks = tokens // MED
    give = pltpu.make_async_copy(hand_ref, hand_hbm, sem.at[chunks])
    give.start()
    scale = lax.rsqrt(energy_ref[...] / width + 1e-05)
    scale = jnp.transpose(jnp.broadcast_to(scale, (LANES, tokens)))
    copies = []
    for c in range(chunks):
        rows = slice(c * MED, (c + 1) * MED)
        for g in range(channels // LANES):
            lanes = slice(g * LANES, (g + 1) * LANES)
            obuf[rows, lanes] = (gated_ref[rows, lanes] * scale[rows] * gain_ref[:, lanes]).astype(BF16)
        copy = pltpu.make_async_copy(obuf.at[pl.ds(c * MED, MED)], out_hbm.at[pl.ds(c * MED, MED)], sem.at[c])
        copy.start()
        copies.append(copy)
    for copy in copies:
        copy.wait()
    give.wait()


def per_device(query_rows, key_rows, value_rows, residues, decay_rates, medium_taps, out_gain, reader_plan):
    tokens, channels = query_rows.shape
    tiles = channels // LANES
    groups = tiles * 8
    seq = lax.axis_size("seq")
    nz = math.isqrt(seq)
    ny = seq // nz
    nc = lax.axis_size("chan")
    cfg = (ny, nz, nc, tiles, tokens)
    chunks = tokens // MED
    vm = pltpu.VMEM
    dma = pltpu.SemaphoreType.DMA
    scratch = [
        vm((tokens, channels), BF16), vm((tokens, channels), BF16), vm((tokens, channels), BF16),
        vm((tokens, channels), BF16), vm((MED, channels), BF16),
        vm((MODES, groups), F32), vm((MODES, groups), F32), vm((groups, MED), F32), vm((NB + 1, groups), jnp.int32),
        vm((channels, LANES), F32), vm((tiles, LANES, LANES), BF16),
        vm((MODES, channels), F32), vm((groups, LANES), F32), vm((groups, LANES), F32),
        vm((tiles, 2 * LANES, 8 * LANES), BF16), vm((tokens, channels), BF16),
        vm((2, 8 * LANES, 3 * LANES), BF16),
        vm((chunks, MODES, channels), F32),
        vm((nz, MODES, LANES), BF16), vm((nz, MODES, LANES), BF16), vm((nz, MODES, LANES), F32),
        vm((MODES, LANES), BF16), vm((ny, MODES, LANES), BF16),
        vm((nz, 2, MODES, LANES), BF16), vm((nz, 2, MODES, LANES), BF16),
        vm((NB * groups, 2 * LANES), F32), vm((nz - 1, ny, SLOTS, 2 * LANES), BF16),
        vm((ny, SLOTS, 2 * LANES), BF16), vm((SLOTS, 2 * LANES), BF16),
        vm((1, tokens), F32), vm((nc, 1, tokens), F32),
        dma((4, chunks)),
        dma, dma, dma, dma, dma, dma, dma, dma, dma, dma, dma, dma, dma, dma,
    ]
    hbm = pl.BlockSpec(memory_space=pltpu.HBM)
    vmem = pl.BlockSpec(memory_space=pltpu.VMEM)
    gated, hand, energy = pl.pallas_call(
        functools.partial(kernel, cfg),
        name="hyena",
        out_shape=(
            jax.ShapeDtypeStruct((tokens, channels), F32),
            jax.ShapeDtypeStruct((10, MODES, GW), F32),
            jax.ShapeDtypeStruct((1, tokens), F32),
        ),
        in_specs=[hbm] * 7,
        out_specs=(vmem, vmem, vmem),
        scratch_shapes=scratch,
        compiler_params=pltpu.CompilerParams(
            collective_id=0, has_side_effects=True, vmem_limit_bytes=48 * 1024 * 1024),
    )(*[pltpu.with_memory_space_constraint(a, pltpu.HBM) for a in (query_rows, key_rows, value_rows, residues.T, decay_rates.T, medium_taps, reader_plan.T)])
    return pl.pallas_call(
        functools.partial(finish, nc * channels),
        name="finish",
        out_shape=(
            jax.ShapeDtypeStruct((tokens, channels), BF16),
            jax.ShapeDtypeStruct((10, MODES, GW), F32),
        ),
        in_specs=[vmem] * 4,
        out_specs=(hbm, hbm),
        scratch_shapes=[vm((tokens, channels), BF16), dma((chunks + 1,))],
        compiler_params=pltpu.CompilerParams(vmem_limit_bytes=48 * 1024 * 1024),
    )(gated, hand, energy, out_gain.reshape(1, channels))


def solution(mesh):
    placed = (
        P("seq", "chan"),
        P("seq", "chan"),
        P("seq", "chan"),
        P("chan", None),
        P("chan", None),
        P("chan", None),
        P("chan"),
        P("chan", None),
    )
    return jax.shard_map(
        per_device,
        mesh=mesh,
        in_specs=placed,
        out_specs=(P("seq", "chan"), P("seq", None, "chan")),
        check_vma=False,
    )
```

```python
import functools
import math

import jax
import jax.numpy as jnp
from jax import lax
from jax.experimental import pallas as pl
from jax.experimental.pallas import tpu as pltpu
from jax.sharding import PartitionSpec as P

D = 8192
GW = 16
MODES = 16
MED = 128
NB = 8
SLOTS = 16
PIECE = 64
LANES = 128
F32 = jnp.float32
BF16 = jnp.bfloat16
MESH = pl.DeviceIdType.MESH


def iota(shape, axis):
    return lax.broadcasted_iota(jnp.int32, shape, axis)


def split(x, parts):
    out = []
    for _ in range(parts):
        piece = x.astype(BF16)
        out.append(piece)
        x = x - piece.astype(F32)
    return out


def one_minus_exp_neg(x):
    small = x * (1.0 - x * (1 / 2) * (1.0 - x * (1 / 3) * (1.0 - x * (1 / 4) * (
        1.0 - x * (1 / 5) * (1.0 - x * (1 / 6) * (1.0 - x * (1 / 7)))))))
    return jnp.where(x < 0.1, small, 1.0 - jnp.exp(-x))


LOG2E = 1.4426950408889634
LN2 = 0.6931471805599453


def dot(a, b):
    return jnp.dot(a, b, preferred_element_type=F32)


def swap_blocks(x):
    n = x.shape[0]
    sub = iota((n, 8, LANES), 1)
    blk = iota((n, 8, LANES), 2) // GW
    gap = (blk - sub + 8) % 8
    out = x
    for d in range(1, 8):
        moved = pltpu.roll(pltpu.roll(x, 8 - d, 1), GW * d, 2)
        out = jnp.where(gap == d, moved, out)
    return out


def kernel(cfg, q_hbm, k_hbm, v_hbm, res_hbm, lam_hbm, taps_hbm, plan_hbm, gain_hbm,
           local, hand_ref, energy_ref,
           kbuf, vbuf, qbuf, xbuf, hbuf, lam_v, res_v, taps_v, plan_v, gain_v, lamc, eb, lame, gh, gt, tmat, smat, rhs, st,
           a1s, a1r, pre, a2s, a2r, a3s, a3r, items, pk, row, tin, es, er,
           in_sem, s1, r1, s2, r2, s3, r3, sx, rx, sh, rh, sp, rp, sf, rf):
    ny, nz, nc, tiles, tokens = cfg
    groups = tiles * 8
    chunks = tokens // MED
    me = lax.axis_index("seq")
    ch = lax.axis_index("chan")
    y = me // nz
    z = me % nz
    last = ny * nz - 1

    def order(n):
        return sorted(range(1, n), key=lambda d: -min(d, n - d))

    barrier = pltpu.get_barrier_semaphore()

    def greet(seq, chan):
        pl.semaphore_signal(barrier, inc=1, device_id=(seq, chan), device_id_type=MESH)

    for d in order(nz):
        greet(y * nz + (z + d) % nz, ch)
    for d in order(ny):
        greet(((y + d) % ny) * nz + z, ch)
    for d in order(nc):
        greet(me, (ch + d) % nc)
    wraps_on = (z == nz - 1) & (y < ny - 1)
    wraps_in = (z == 0) & (y > 0)

    @pl.when(wraps_on)
    def _():
        greet(me + 1, ch)

    @pl.when(wraps_in)
    def _():
        greet(me - 1, ch)

    def fetch(src, dst, a, b):
        return pltpu.make_async_copy(src, dst, in_sem.at[a, b])

    def fetch_rows(c):
        rows = pl.ds(c * MED, MED)
        return (fetch(k_hbm.at[rows], kbuf.at[rows], 0, c), fetch(v_hbm.at[rows], vbuf.at[rows], 1, c))

    get_lam = fetch(lam_hbm, lam_v, 2, 0)
    get_res = fetch(res_hbm, res_v, 2, 1)
    get_taps = fetch(taps_hbm, taps_v, 2, 2)
    get_plan = fetch(plan_hbm, plan_v, 3, 0)
    get_q = fetch(q_hbm, qbuf, 3, 1)
    get_gain = fetch(gain_hbm, gain_v, 3, 2)
    get_lam.start()
    for c in range(chunks):
        for copy in fetch_rows(c):
            copy.start()
    get_res.start()
    get_taps.start()
    get_plan.start()
    get_q.start()
    get_gain.start()

    get_lam.wait()
    lam_t = lam_v[...]
    lam2 = lam_t * LOG2E
    own16 = iota((MODES, LANES), 1) // GW
    lane128 = iota((LANES, LANES), 1)
    back = (iota((MODES, LANES), 1) - LANES).astype(F32)
    for g in range(tiles):
        spread = jnp.zeros((MODES, LANES), F32)
        for k in range(8):
            f = g * 8 + k
            col = jnp.broadcast_to(lam2[:, f:f + 1], (MODES, LANES))
            spread = jnp.where(own16 == k, col, spread)
            lamc[f * MODES:(f + 1) * MODES, :] = col
            eb[g, k * MODES:(k + 1) * MODES, :] = jnp.exp2(col * back).astype(BF16)
        lame[:, g * LANES:(g + 1) * LANES] = spread

    for c in range(chunks):
        rows = pl.ds(c * MED, MED)
        for copy in fetch_rows(c):
            copy.wait()
        xbuf[rows, :] = kbuf[rows, :] * vbuf[rows, :]

    for g in range(tiles):
        lanes = slice(g * LANES, (g + 1) * LANES)
        total = None
        d128 = jnp.exp2(lame[:, lanes] * (-float(MED)))
        both = jnp.concatenate([xbuf[c * MED:(c + 1) * MED, lanes] for c in range(chunks)], axis=1)
        raw = dot(eb[g], both)
        for c in range(chunks):
            part = jnp.zeros((MODES, LANES), F32)
            for k in range(8):
                piece = raw[k * MODES:(k + 1) * MODES, c * LANES:(c + 1) * LANES]
                part = jnp.where(own16 == k, piece, part)
            total = part if total is None else total * d128 + part
            if c < chunks - 1:
                st[c, :, lanes] = total
        a1s[g] = total.astype(BF16)

    extra = wraps_on.astype(jnp.int32) + wraps_in.astype(jnp.int32)
    pl.semaphore_wait(barrier, (nz - 1) + (ny - 1) + (nc - 1) + extra)

    def remote(src, dst, send, recv, seq, chan):
        return pltpu.make_async_remote_copy(
            src_ref=src, dst_ref=dst, send_sem=send, recv_sem=recv,
            device_id=(seq, chan), device_id_type=MESH)

    def settle(ref, sem):
        pltpu.make_async_copy(ref, ref, sem).wait()

    for d in order(nz):
        to = (z + d) % nz
        copy = remote(a1s.at[to], a1r.at[z], s1, r1, y * nz + to, ch)
        copy.start()
    a1r[z] = a1s[z]

    def halo():
        return remote(xbuf.at[pl.ds(tokens - MED, MED)], hbuf, sh, rh, me + 1, ch)

    get_plan.wait()
    plan = jnp.transpose(plan_v[...].astype(F32))
    tri = (iota((groups, groups), 1) < iota((groups, groups), 0)).astype(BF16)

    @pl.when(me == last)
    def _():
        who = iota((groups, LANES), 1).astype(F32)
        hits = jnp.zeros((groups, LANES), F32)
        for b in range(NB + 1):
            hits = hits + (plan[:, b:b + 1] == who).astype(F32)
        before = dot(tri, hits.astype(BF16))
        slots = jnp.full((groups, LANES), -1.0, F32)
        for b in range(NB):
            reader = plan[:, b:b + 1]
            rank = jnp.sum(jnp.where(reader == who, before, 0.0), axis=1, keepdims=True)
            down = jnp.floor((reader + 0.5) * (1.0 / nz))
            place = (reader - down * nz) * ny + down
            slots = jnp.where(who == b, place * SLOTS + rank, slots)
        slots_t = jnp.transpose(slots)
        for b in range(NB):
            for half in range(2):
                for g in range(tiles):
                    tile = xbuf[tokens - MED + b * MODES:tokens - MED + (b + 1) * MODES,
                                g * LANES:(g + 1) * LANES].astype(F32)[half * 8:half * 8 + 8]
                    items[b * groups + g * 8:b * groups + g * 8 + 8,
                          half * LANES:(half + 1) * LANES] = swap_blocks(tile[None])[0]
        wanted = [jnp.concatenate([slots_t[b:b + 1, 0:groups] for b in range(4 * i, 4 * i + 4)], axis=1)
                  for i in range(NB // 4)]
        for part in range(nz):
            count = ny * SLOTS
            base = part * count
            acc = jnp.zeros((count, 2 * LANES), F32)
            target = (iota((count, 4 * groups), 0) + base).astype(F32)
            for b in range(NB // 4):
                pick = (target == wanted[b]).astype(BF16)
                acc = acc + dot(pick, items[4 * b * groups:4 * (b + 1) * groups, :].astype(BF16))
            packed = acc.astype(BF16).reshape(ny, SLOTS, 2 * LANES)
            if part == nz - 1:
                row[...] = packed
            else:
                pk[part] = packed

    def pack_copy(part):
        return remote(pk.at[part], row, sp, rp, (ny - 1) * nz + part, ch)

    @pl.when(me == last)
    def _():
        for part in range(nz - 1):
            pack_copy(part).start()

    get_res.wait()
    get_taps.wait()
    weight_t = res_v[...] * jnp.sqrt(one_minus_exp_neg(2.0 * lam_t))
    perm = (iota((LANES, LANES), 0) == (LANES - lane128) % LANES).astype(BF16)
    flipped = dot(jnp.concatenate(split(taps_v[...], 3), axis=0), perm)
    flipped = flipped[0:groups] + flipped[groups:2 * groups] + flipped[2 * groups:3 * groups]
    gt[...] = flipped
    zero16 = iota((MODES, LANES), 1) == 0
    for g in range(tiles):
        sums = []
        for k in range(8):
            f = g * 8 + k
            w = jnp.broadcast_to(weight_t[:, f:f + 1], (MODES, LANES))
            e = jnp.exp2(lamc[f * MODES:(f + 1) * MODES, :] * back)
            sums.append(jnp.sum(jnp.where(zero16, w, w * e), axis=0, keepdims=True))
        gh[g * 8:(g + 1) * 8, :] = jnp.concatenate(sums, axis=0) + flipped[g * 8:(g + 1) * 8]

    def conv_build(g, side):
        lanes = pl.ds(pl.multiple_of(g * LANES, LANES), LANES)
        rows8 = pl.ds(pl.multiple_of(g * 8, 8), 8)
        full = gh[rows8, :]
        taps = gt[rows8, :]
        lower = iota((LANES, LANES), 1) <= iota((LANES, LANES), 0)
        which = iota((MED, LANES), 1) // GW
        x0 = xbuf[0:MED, lanes]
        x1 = xbuf[MED:2 * MED, lanes]
        x2 = xbuf[2 * MED:3 * MED, lanes]
        for k in range(8):
            a = pltpu.roll(jnp.broadcast_to(full[k:k + 1], (LANES, LANES)), 0, 1, stride=1, stride_axis=0)
            b = pltpu.roll(jnp.broadcast_to(taps[k:k + 1], (LANES, LANES)), 0, 1, stride=1, stride_axis=0)
            cols = slice(k * LANES, (k + 1) * LANES)
            tmat[g, 0:LANES, cols] = jnp.where(lower, a, 0.0).astype(BF16)
            tmat[g, LANES:2 * LANES, cols] = jnp.where(lower, 0.0, b).astype(BF16)
            keep = (which == k).astype(BF16)
            rhs[side, cols, 0:LANES] = x0 * keep
            rhs[side, cols, LANES:2 * LANES] = x1 * keep
            rhs[side, cols, 2 * LANES:3 * LANES] = x2 * keep

    def conv_apply(g, side):
        lanes = pl.ds(pl.multiple_of(g * LANES, LANES), LANES)
        out = dot(tmat[g], rhs[side, :, 0:2 * LANES])
        out2 = dot(tmat[g, 0:LANES, :], rhs[side, :, 2 * LANES:3 * LANES])
        local[0:MED, lanes] = out[0:LANES, 0:LANES]
        local[MED:2 * MED, lanes] = out[0:LANES, LANES:2 * LANES] + out[LANES:2 * LANES, 0:LANES]
        local[2 * MED:3 * MED, lanes] = out2 + out[LANES:2 * LANES, LANES:2 * LANES]

    def conv_pair(p, carry):
        conv_build(2 * p, 0)
        conv_build(2 * p + 1, 1)
        conv_apply(2 * p, 0)
        conv_apply(2 * p + 1, 1)
        return carry

    pairs = tiles // 2
    early = jnp.where(me == last, pairs // 4, 3 * pairs // 4)
    lax.fori_loop(0, early, conv_pair, 0)

    mine = pl.ds(pl.multiple_of(z * LANES, LANES), LANES)
    lam_s = lame[:, mine]
    d_dev = jnp.exp2(lam_s * (-float(tokens)))
    settle(a1r.at[pl.ds(0, nz - 1)], r1)
    run = jnp.zeros((MODES, LANES), F32)
    for i in range(nz):
        pre[i] = run
        run = run * d_dev + a1r[i].astype(F32)
    a2s[...] = run.astype(BF16)

    for d in order(ny):
        to = (y + d) % ny
        copy = remote(a2s, a2r.at[y], s2, r2, to * nz + z, ch)
        copy.start()
    a2r[y] = a2s[...]

    @pl.when(me < last)
    def _():
        halo().start()

    lax.fori_loop(early, pairs, conv_pair, 0)

    for g in range(tiles):
        lanes = slice(g * LANES, (g + 1) * LANES)
        rates = lamc[lanes, :]
        weight = jnp.concatenate(
            [jnp.broadcast_to(weight_t[:, f:f + 1], (MODES, LANES)) for f in range(g * 8, g * 8 + 8)], axis=0)
        at = lane128.astype(F32)
        for c in range(chunks):
            s = weight * jnp.exp2(-rates * (at + float(c * MED)))
            smat[c * MED:(c + 1) * MED, lanes] = jnp.transpose(s).astype(BF16)
        same = (iota((LANES, LANES), 0) // MODES) == (iota((LANES, LANES), 1) // GW)
        pieces = []
        for c in range(chunks - 1):
            state = jnp.concatenate([st[c, :, lanes]] * 8, axis=0)
            pieces.append(jnp.where(same, state, 0.0))
        hi, lo = split(jnp.concatenate(pieces, axis=1), 2)
        factor = smat[0:MED, lanes]
        out = dot(jnp.concatenate([factor, factor], axis=1), jnp.concatenate([hi, lo], axis=0))
        for c in range(chunks - 1):
            rows = slice((c + 1) * MED, (c + 2) * MED)
            local[rows, lanes] = local[rows, lanes] + out[:, c * LANES:(c + 1) * LANES]

    d_row = jnp.exp2(lam_s * (-float(tokens * nz)))
    settle(a2r.at[pl.ds(0, ny - 1)], r2)
    run = jnp.zeros((MODES, LANES), F32)
    above = jnp.zeros((MODES, LANES), F32)
    for i in range(ny):
        above = jnp.where(y == i, run, above)
        run = run * d_row + a2r[i].astype(F32)
    norm_s = jnp.sqrt(one_minus_exp_neg(lam_s * (2.0 * LN2)))
    final = (run * norm_s).astype(BF16)
    for i in range(nz):
        a3s[i, 0] = (above + pre[i]).astype(BF16)
        a3s[i, 1] = final
        above = above * d_dev

    for d in order(nz):
        to = (z + d) % nz
        copy = remote(a3s.at[to], a3r.at[z], s3, r3, y * nz + to, ch)
        copy.start()
    a3r[z] = a3s[z]

    def hop_copy(to):
        return remote(row.at[to], tin, sf, rf, to * nz + z, ch)

    @pl.when((y == ny - 1) & (me != last))
    def _():
        remote(pk.at[0], row, sp, rp, me, ch).wait_recv()

    @pl.when(y == ny - 1)
    def _():
        for to in range(ny - 1):
            hop_copy(to).start()
        tin[...] = row[ny - 1]

    @pl.when(me > 0)
    def _():
        remote(xbuf.at[pl.ds(tokens - MED, MED)], hbuf, sh, rh, me, ch).wait_recv()

        def halo_tile(g, carry):
            lanes = pl.ds(pl.multiple_of(g * LANES, LANES), LANES)
            which = iota((MED, LANES), 1) // GW
            xh = hbuf[:, lanes]
            for k in range(8):
                rhs[0, k * LANES:(k + 1) * LANES, 0:LANES] = xh * (which == k).astype(BF16)
            out = dot(tmat[g, LANES:2 * LANES, :], rhs[0, :, 0:LANES])
            local[0:MED, lanes] = local[0:MED, lanes] + out
            return carry

        lax.fori_loop(0, tiles, halo_tile, 0)

    get_q.wait()
    get_gain.wait()
    settle(a3r.at[pl.ds(0, nz - 1)], r3)

    power = jnp.zeros((tokens, LANES), F32)
    wide = 2 * LANES
    same2 = ((iota((wide, wide), 0) // MODES) == (iota((wide, wide), 1) // GW)).astype(BF16)
    for g in range(tiles // 2):
        lanes = slice(g * wide, (g + 1) * wide)
        state = jnp.concatenate([a3r[2 * g, 0], a3r[2 * g + 1, 0]], axis=1)
        spread = jnp.concatenate([state] * 16, axis=0) * same2
        cross = dot(smat[:, lanes], spread)
        gated = qbuf[:, lanes].astype(F32) * (local[:, lanes] + cross)
        local[:, lanes] = gated
        sq = gated * gated
        power = power + sq[:, 0:LANES] + sq[:, LANES:wide]
    es[...] = jnp.sum(jnp.transpose(power), axis=0, keepdims=True)

    for d in order(nc):
        to = (ch + d) % nc
        copy = remote(es, er.at[ch], sx, rx, me, to)
        copy.start()
    er[ch] = es[...]

    mine_hit = (plan == me.astype(F32)).astype(F32)
    hit = jnp.sum(mine_hit, axis=1, keepdims=True)
    before = dot(tri, jnp.broadcast_to(hit, (groups, 2 * LANES)).astype(BF16))
    slot = (iota((groups, 2 * LANES), 1) // GW).astype(F32)
    wants = jnp.where(before == slot, mine_hit[:, NB:NB + 1], 0.0).astype(BF16)
    picked = jnp.zeros((MODES, 2 * LANES), F32)
    delta = ((iota((LANES, 2 * LANES), 0) % GW) == (iota((LANES, 2 * LANES), 1) % GW)).astype(F32)
    for g in range(tiles):
        rep = ((iota((LANES, groups), 0) // GW + g * 8) == iota((LANES, groups), 1)).astype(BF16)
        choose = (dot(rep, wants) * delta).astype(BF16)
        picked = picked + dot(a3r[g, 1], choose)

    @pl.when(y != ny - 1)
    def _():
        remote(row.at[0], tin, sf, rf, me, ch).wait_recv()

    tails = tin[...].astype(F32)
    for a in range(2):
        for b in range(2):
            block = swap_blocks(tails[8 * a:8 * a + 8, b * LANES:(b + 1) * LANES][None])[0]
            block = block + picked[8 * b:8 * b + 8, a * LANES:(a + 1) * LANES]
            for k in range(8):
                j = a * 8 + k
                if j < 10:
                    hand_ref[j, 8 * b:8 * b + 8, :] = block[:, k * GW:(k + 1) * GW]

    settle(a1s.at[pl.ds(0, nz - 1)], s1)
    settle(a2r.at[pl.ds(0, ny - 1)], s2)
    settle(a3s.at[pl.ds(0, nz - 1)], s3)

    @pl.when(me < last)
    def _():
        halo().wait_send()

    @pl.when(me == last)
    def _():
        settle(pk, sp)

    @pl.when(y == ny - 1)
    def _():
        settle(row.at[pl.ds(0, ny - 1)], sf)

    for g in range(tiles):
        lanes = slice(g * LANES, (g + 1) * LANES)
        local[:, lanes] = local[:, lanes] * gain_v[:, lanes]

    settle(er.at[pl.ds(0, nc - 1)], rx)
    energy = er[0]
    for i in range(1, nc):
        energy = energy + er[i]
    energy_ref[...] = energy
    settle(er.at[pl.ds(0, nc - 1)], sx)


def finish(width, gated_ref, hand_ref, energy_ref, out_hbm, hand_hbm, obuf, sem):
    tokens, channels = gated_ref.shape
    chunks = tokens // PIECE
    give = pltpu.make_async_copy(hand_ref, hand_hbm, sem.at[chunks])
    give.start()
    scale = lax.rsqrt(energy_ref[...] / width + 1e-05)
    scale = jnp.transpose(jnp.broadcast_to(scale, (LANES, tokens)))
    copies = []
    for c in range(chunks):
        rows = slice(c * PIECE, (c + 1) * PIECE)
        for g in range(channels // LANES):
            lanes = slice(g * LANES, (g + 1) * LANES)
            obuf[rows, lanes] = (gated_ref[rows, lanes] * scale[rows]).astype(BF16)
        copy = pltpu.make_async_copy(obuf.at[pl.ds(c * PIECE, PIECE)], out_hbm.at[pl.ds(c * PIECE, PIECE)], sem.at[c])
        copy.start()
        copies.append(copy)
    for copy in copies:
        copy.wait()
    give.wait()


def per_device(query_rows, key_rows, value_rows, residues, decay_rates, medium_taps, out_gain, reader_plan):
    tokens, channels = query_rows.shape
    tiles = channels // LANES
    groups = tiles * 8
    seq = lax.axis_size("seq")
    nz = math.isqrt(seq)
    ny = seq // nz
    nc = lax.axis_size("chan")
    cfg = (ny, nz, nc, tiles, tokens)
    chunks = tokens // MED
    vm = pltpu.VMEM
    dma = pltpu.SemaphoreType.DMA
    scratch = [
        vm((tokens, channels), BF16), vm((tokens, channels), BF16), vm((tokens, channels), BF16),
        vm((tokens, channels), BF16), vm((MED, channels), BF16),
        vm((MODES, groups), F32), vm((MODES, groups), F32), vm((groups, MED), F32), vm((NB + 1, groups), jnp.int32), vm((1, channels), F32),
        vm((channels, LANES), F32), vm((tiles, LANES, LANES), BF16),
        vm((MODES, channels), F32), vm((groups, LANES), F32), vm((groups, LANES), F32),
        vm((tiles, 2 * LANES, 8 * LANES), BF16), vm((tokens, channels), BF16),
        vm((2, 8 * LANES, 3 * LANES), BF16),
        vm((chunks, MODES, channels), F32),
        vm((nz, MODES, LANES), BF16), vm((nz, MODES, LANES), BF16), vm((nz, MODES, LANES), F32),
        vm((MODES, LANES), BF16), vm((ny, MODES, LANES), BF16),
        vm((nz, 2, MODES, LANES), BF16), vm((nz, 2, MODES, LANES), BF16),
        vm((NB * groups, 2 * LANES), F32), vm((nz - 1, ny, SLOTS, 2 * LANES), BF16),
        vm((ny, SLOTS, 2 * LANES), BF16), vm((SLOTS, 2 * LANES), BF16),
        vm((1, tokens), F32), vm((nc, 1, tokens), F32),
        dma((4, chunks)),
        dma, dma, dma, dma, dma, dma, dma, dma, dma, dma, dma, dma, dma, dma,
    ]
    hbm = pl.BlockSpec(memory_space=pltpu.HBM)
    vmem = pl.BlockSpec(memory_space=pltpu.VMEM)
    gated, hand, energy = pl.pallas_call(
        functools.partial(kernel, cfg),
        name="hyena",
        out_shape=(
            jax.ShapeDtypeStruct((tokens, channels), F32),
            jax.ShapeDtypeStruct((10, MODES, GW), F32),
            jax.ShapeDtypeStruct((1, tokens), F32),
        ),
        in_specs=[hbm] * 8,
        out_specs=(vmem, vmem, vmem),
        scratch_shapes=scratch,
        compiler_params=pltpu.CompilerParams(
            collective_id=0, has_side_effects=True, vmem_limit_bytes=48 * 1024 * 1024),
    )(*[pltpu.with_memory_space_constraint(a, pltpu.HBM) for a in (query_rows, key_rows, value_rows, residues.T, decay_rates.T, medium_taps, reader_plan.T, out_gain.reshape(1, channels))])
    return pl.pallas_call(
        functools.partial(finish, nc * channels),
        name="finish",
        out_shape=(
            jax.ShapeDtypeStruct((tokens, channels), BF16),
            jax.ShapeDtypeStruct((10, MODES, GW), F32),
        ),
        in_specs=[vmem] * 3,
        out_specs=(hbm, hbm),
        scratch_shapes=[vm((tokens, channels), BF16), dma((tokens // PIECE + 1,))],
        compiler_params=pltpu.CompilerParams(vmem_limit_bytes=48 * 1024 * 1024),
    )(gated, hand, energy)


def solution(mesh):
    placed = (
        P("seq", "chan"),
        P("seq", "chan"),
        P("seq", "chan"),
        P("chan", None),
        P("chan", None),
        P("chan", None),
        P("chan"),
        P("chan", None),
    )
    return jax.shard_map(
        per_device,
        mesh=mesh,
        in_specs=placed,
        out_specs=(P("seq", "chan"), P("seq", None, "chan")),
        check_vma=False,
    )
```

```python
import functools
import math

import jax
import jax.numpy as jnp
from jax import lax
from jax.experimental import pallas as pl
from jax.experimental.pallas import tpu as pltpu
from jax.sharding import PartitionSpec as P

D = 8192
GW = 16
MODES = 16
MED = 128
NB = 8
SLOTS = 16
PIECE = 64
LANES = 128
F32 = jnp.float32
BF16 = jnp.bfloat16
MESH = pl.DeviceIdType.MESH


def iota(shape, axis):
    return lax.broadcasted_iota(jnp.int32, shape, axis)


def split(x, parts):
    out = []
    for _ in range(parts):
        piece = x.astype(BF16)
        out.append(piece)
        x = x - piece.astype(F32)
    return out


def one_minus_exp_neg(x):
    small = x * (1.0 - x * (1 / 2) * (1.0 - x * (1 / 3) * (1.0 - x * (1 / 4) * (
        1.0 - x * (1 / 5) * (1.0 - x * (1 / 6) * (1.0 - x * (1 / 7)))))))
    return jnp.where(x < 0.1, small, 1.0 - jnp.exp(-x))


LOG2E = 1.4426950408889634
LN2 = 0.6931471805599453


def dot(a, b):
    return jnp.dot(a, b, preferred_element_type=F32)


def swap_blocks(x):
    n = x.shape[0]
    sub = iota((n, 8, LANES), 1)
    blk = iota((n, 8, LANES), 2) // GW
    gap = (blk - sub + 8) % 8
    out = x
    for d in range(1, 8):
        moved = pltpu.roll(pltpu.roll(x, 8 - d, 1), GW * d, 2)
        out = jnp.where(gap == d, moved, out)
    return out


def kernel(cfg, q_hbm, k_hbm, v_hbm, res_hbm, lam_hbm, taps_hbm, plan_hbm, gain_hbm,
           local, hand_ref, energy_ref,
           kbuf, vbuf, qbuf, xbuf, hbuf, lam_v, res_v, taps_v, plan_v, gain_v, lamc, eb, lame, gh, gt, tmat, smat, rhs, st,
           a1s, a1r, pre, a2s, a2r, a3s, a3r, items, pk, row, tin, es, er,
           in_sem, s1, r1, s2, r2, s3, r3, sx, rx, sh, rh, sp, rp, sf, rf):
    ny, nz, nc, tiles, tokens = cfg
    groups = tiles * 8
    chunks = tokens // MED
    me = lax.axis_index("seq")
    ch = lax.axis_index("chan")
    y = me // nz
    z = me % nz
    last = ny * nz - 1

    def order(n):
        return sorted(range(1, n), key=lambda d: -min(d, n - d))

    barrier = pltpu.get_barrier_semaphore()

    def greet(seq, chan):
        pl.semaphore_signal(barrier, inc=1, device_id=(seq, chan), device_id_type=MESH)

    for d in order(nz):
        greet(y * nz + (z + d) % nz, ch)
    for d in order(ny):
        greet(((y + d) % ny) * nz + z, ch)
    for d in order(nc):
        greet(me, (ch + d) % nc)
    wraps_on = (z == nz - 1) & (y < ny - 1)
    wraps_in = (z == 0) & (y > 0)

    @pl.when(wraps_on)
    def _():
        greet(me + 1, ch)

    @pl.when(wraps_in)
    def _():
        greet(me - 1, ch)

    def fetch(src, dst, a, b):
        return pltpu.make_async_copy(src, dst, in_sem.at[a, b])

    def fetch_rows(c):
        rows = pl.ds(c * MED, MED)
        return (fetch(k_hbm.at[rows], kbuf.at[rows], 0, c), fetch(v_hbm.at[rows], vbuf.at[rows], 1, c))

    get_lam = fetch(lam_hbm, lam_v, 2, 0)
    get_res = fetch(res_hbm, res_v, 2, 1)
    get_taps = fetch(taps_hbm, taps_v, 2, 2)
    get_plan = fetch(plan_hbm, plan_v, 3, 0)
    get_q = fetch(q_hbm, qbuf, 3, 1)
    get_gain = fetch(gain_hbm, gain_v, 3, 2)
    get_lam.start()
    for c in range(chunks):
        for copy in fetch_rows(c):
            copy.start()
    get_res.start()
    get_taps.start()
    get_plan.start()
    get_q.start()
    get_gain.start()

    get_lam.wait()
    lam_t = lam_v[...]
    lam2 = lam_t * LOG2E
    own16 = iota((MODES, LANES), 1) // GW
    lane128 = iota((LANES, LANES), 1)
    back = (iota((MODES, LANES), 1) - LANES).astype(F32)
    for g in range(tiles):
        spread = jnp.zeros((MODES, LANES), F32)
        for k in range(8):
            f = g * 8 + k
            col = jnp.broadcast_to(lam2[:, f:f + 1], (MODES, LANES))
            spread = jnp.where(own16 == k, col, spread)
            lamc[f * MODES:(f + 1) * MODES, :] = col
            eb[g, k * MODES:(k + 1) * MODES, :] = jnp.exp2(col * back).astype(BF16)
        lame[:, g * LANES:(g + 1) * LANES] = spread

    for c in range(chunks):
        rows = pl.ds(c * MED, MED)
        for copy in fetch_rows(c):
            copy.wait()
        xbuf[rows, :] = kbuf[rows, :] * vbuf[rows, :]

    for g in range(tiles):
        lanes = slice(g * LANES, (g + 1) * LANES)
        total = None
        d128 = jnp.exp2(lame[:, lanes] * (-float(MED)))
        both = jnp.concatenate([xbuf[c * MED:(c + 1) * MED, lanes] for c in range(chunks)], axis=1)
        raw = dot(eb[g], both)
        for c in range(chunks):
            part = jnp.zeros((MODES, LANES), F32)
            for k in range(8):
                piece = raw[k * MODES:(k + 1) * MODES, c * LANES:(c + 1) * LANES]
                part = jnp.where(own16 == k, piece, part)
            total = part if total is None else total * d128 + part
            if c < chunks - 1:
                st[c, :, lanes] = total
        a1s[g] = total.astype(BF16)

    extra = wraps_on.astype(jnp.int32) + wraps_in.astype(jnp.int32)
    pl.semaphore_wait(barrier, (nz - 1) + (ny - 1) + (nc - 1) + extra)

    def remote(src, dst, send, recv, seq, chan):
        return pltpu.make_async_remote_copy(
            src_ref=src, dst_ref=dst, send_sem=send, recv_sem=recv,
            device_id=(seq, chan), device_id_type=MESH)

    def settle(ref, sem):
        pltpu.make_async_copy(ref, ref, sem).wait()

    for d in order(nz):
        to = (z + d) % nz
        copy = remote(a1s.at[to], a1r.at[z], s1, r1, y * nz + to, ch)
        copy.start()
    a1r[z] = a1s[z]

    def halo():
        return remote(xbuf.at[pl.ds(tokens - MED, MED)], hbuf, sh, rh, me + 1, ch)

    get_plan.wait()
    plan = jnp.transpose(plan_v[...].astype(F32))
    tri = (iota((groups, groups), 1) < iota((groups, groups), 0)).astype(BF16)

    @pl.when(me == last)
    def _():
        who = iota((groups, LANES), 1).astype(F32)
        hits = jnp.zeros((groups, LANES), F32)
        for b in range(NB + 1):
            hits = hits + (plan[:, b:b + 1] == who).astype(F32)
        before = dot(tri, hits.astype(BF16))
        slots = jnp.full((groups, LANES), -1.0, F32)
        for b in range(NB):
            reader = plan[:, b:b + 1]
            rank = jnp.sum(jnp.where(reader == who, before, 0.0), axis=1, keepdims=True)
            down = jnp.floor((reader + 0.5) * (1.0 / nz))
            place = (reader - down * nz) * ny + down
            slots = jnp.where(who == b, place * SLOTS + rank, slots)
        slots_t = jnp.transpose(slots)
        for b in range(NB):
            for half in range(2):
                for g in range(tiles):
                    tile = xbuf[tokens - MED + b * MODES:tokens - MED + (b + 1) * MODES,
                                g * LANES:(g + 1) * LANES].astype(F32)[half * 8:half * 8 + 8]
                    items[b * groups + g * 8:b * groups + g * 8 + 8,
                          half * LANES:(half + 1) * LANES] = swap_blocks(tile[None])[0]
        wanted = [jnp.concatenate([slots_t[b:b + 1, 0:groups] for b in range(4 * i, 4 * i + 4)], axis=1)
                  for i in range(NB // 4)]
        for part in range(nz):
            count = ny * SLOTS
            base = part * count
            acc = jnp.zeros((count, 2 * LANES), F32)
            target = (iota((count, 4 * groups), 0) + base).astype(F32)
            for b in range(NB // 4):
                pick = (target == wanted[b]).astype(BF16)
                acc = acc + dot(pick, items[4 * b * groups:4 * (b + 1) * groups, :].astype(BF16))
            packed = acc.astype(BF16).reshape(ny, SLOTS, 2 * LANES)
            if part == nz - 1:
                row[...] = packed
            else:
                pk[part] = packed

    def pack_copy(part):
        return remote(pk.at[part], row, sp, rp, (ny - 1) * nz + part, ch)

    @pl.when(me == last)
    def _():
        for part in range(nz - 1):
            pack_copy(part).start()

    get_res.wait()
    get_taps.wait()
    weight_t = res_v[...] * jnp.sqrt(one_minus_exp_neg(2.0 * lam_t))
    perm = (iota((LANES, LANES), 0) == (LANES - lane128) % LANES).astype(BF16)
    flipped = dot(jnp.concatenate(split(taps_v[...], 3), axis=0), perm)
    flipped = flipped[0:groups] + flipped[groups:2 * groups] + flipped[2 * groups:3 * groups]
    gt[...] = flipped
    zero16 = iota((MODES, LANES), 1) == 0
    for g in range(tiles):
        sums = []
        for k in range(8):
            f = g * 8 + k
            w = jnp.broadcast_to(weight_t[:, f:f + 1], (MODES, LANES))
            e = jnp.exp2(lamc[f * MODES:(f + 1) * MODES, :] * back)
            sums.append(jnp.sum(jnp.where(zero16, w, w * e), axis=0, keepdims=True))
        gh[g * 8:(g + 1) * 8, :] = jnp.concatenate(sums, axis=0) + flipped[g * 8:(g + 1) * 8]

    def conv_build(g, side):
        lanes = pl.ds(pl.multiple_of(g * LANES, LANES), LANES)
        rows8 = pl.ds(pl.multiple_of(g * 8, 8), 8)
        full = gh[rows8, :]
        taps = gt[rows8, :]
        lower = iota((LANES, LANES), 1) <= iota((LANES, LANES), 0)
        which = iota((MED, LANES), 1) // GW
        x0 = xbuf[0:MED, lanes]
        x1 = xbuf[MED:2 * MED, lanes]
        x2 = xbuf[2 * MED:3 * MED, lanes]
        for k in range(8):
            a = pltpu.roll(jnp.broadcast_to(full[k:k + 1], (LANES, LANES)), 0, 1, stride=1, stride_axis=0)
            b = pltpu.roll(jnp.broadcast_to(taps[k:k + 1], (LANES, LANES)), 0, 1, stride=1, stride_axis=0)
            cols = slice(k * LANES, (k + 1) * LANES)
            tmat[g, 0:LANES, cols] = jnp.where(lower, a, 0.0).astype(BF16)
            tmat[g, LANES:2 * LANES, cols] = jnp.where(lower, 0.0, b).astype(BF16)
            keep = (which == k).astype(BF16)
            rhs[side, cols, 0:LANES] = x0 * keep
            rhs[side, cols, LANES:2 * LANES] = x1 * keep
            rhs[side, cols, 2 * LANES:3 * LANES] = x2 * keep

    def conv_apply(g, side):
        lanes = pl.ds(pl.multiple_of(g * LANES, LANES), LANES)
        out = dot(tmat[g], rhs[side, :, 0:2 * LANES])
        out2 = dot(tmat[g, 0:LANES, :], rhs[side, :, 2 * LANES:3 * LANES])
        local[0:MED, lanes] = out[0:LANES, 0:LANES]
        local[MED:2 * MED, lanes] = out[0:LANES, LANES:2 * LANES] + out[LANES:2 * LANES, 0:LANES]
        local[2 * MED:3 * MED, lanes] = out2 + out[LANES:2 * LANES, LANES:2 * LANES]

    def conv_pair(p, carry):
        conv_build(2 * p, 0)
        conv_build(2 * p + 1, 1)
        conv_apply(2 * p, 0)
        conv_apply(2 * p + 1, 1)
        return carry

    pairs = tiles // 2
    early = jnp.where(me == last, pairs // 4, pairs // 2)
    lax.fori_loop(0, early, conv_pair, 0)

    mine = pl.ds(pl.multiple_of(z * LANES, LANES), LANES)
    lam_s = lame[:, mine]
    d_dev = jnp.exp2(lam_s * (-float(tokens)))
    settle(a1r.at[pl.ds(0, nz - 1)], r1)
    run = jnp.zeros((MODES, LANES), F32)
    for i in range(nz):
        pre[i] = run
        run = run * d_dev + a1r[i].astype(F32)
    a2s[...] = run.astype(BF16)

    for d in order(ny):
        to = (y + d) % ny
        copy = remote(a2s, a2r.at[y], s2, r2, to * nz + z, ch)
        copy.start()
    a2r[y] = a2s[...]

    @pl.when(me < last)
    def _():
        halo().start()

    lax.fori_loop(early, pairs, conv_pair, 0)

    for g in range(tiles):
        lanes = slice(g * LANES, (g + 1) * LANES)
        rates = lamc[lanes, :]
        weight = jnp.concatenate(
            [jnp.broadcast_to(weight_t[:, f:f + 1], (MODES, LANES)) for f in range(g * 8, g * 8 + 8)], axis=0)
        at = lane128.astype(F32)
        for c in range(chunks):
            s = weight * jnp.exp2(-rates * (at + float(c * MED)))
            smat[c * MED:(c + 1) * MED, lanes] = jnp.transpose(s).astype(BF16)
        same = (iota((LANES, LANES), 0) // MODES) == (iota((LANES, LANES), 1) // GW)
        pieces = []
        for c in range(chunks - 1):
            state = jnp.concatenate([st[c, :, lanes]] * 8, axis=0)
            pieces.append(jnp.where(same, state, 0.0))
        hi, lo = split(jnp.concatenate(pieces, axis=1), 2)
        factor = smat[0:MED, lanes]
        out = dot(jnp.concatenate([factor, factor], axis=1), jnp.concatenate([hi, lo], axis=0))
        for c in range(chunks - 1):
            rows = slice((c + 1) * MED, (c + 2) * MED)
            local[rows, lanes] = local[rows, lanes] + out[:, c * LANES:(c + 1) * LANES]

    d_row = jnp.exp2(lam_s * (-float(tokens * nz)))
    settle(a2r.at[pl.ds(0, ny - 1)], r2)
    run = jnp.zeros((MODES, LANES), F32)
    above = jnp.zeros((MODES, LANES), F32)
    for i in range(ny):
        above = jnp.where(y == i, run, above)
        run = run * d_row + a2r[i].astype(F32)
    norm_s = jnp.sqrt(one_minus_exp_neg(lam_s * (2.0 * LN2)))
    final = (run * norm_s).astype(BF16)
    for i in range(nz):
        a3s[i, 0] = (above + pre[i]).astype(BF16)
        a3s[i, 1] = final
        above = above * d_dev

    for d in order(nz):
        to = (z + d) % nz
        copy = remote(a3s.at[to], a3r.at[z], s3, r3, y * nz + to, ch)
        copy.start()
    a3r[z] = a3s[z]

    def hop_copy(to):
        return remote(row.at[to], tin, sf, rf, to * nz + z, ch)

    @pl.when((y == ny - 1) & (me != last))
    def _():
        remote(pk.at[0], row, sp, rp, me, ch).wait_recv()

    @pl.when(y == ny - 1)
    def _():
        for to in range(ny - 1):
            hop_copy(to).start()
        tin[...] = row[ny - 1]

    @pl.when(me > 0)
    def _():
        remote(xbuf.at[pl.ds(tokens - MED, MED)], hbuf, sh, rh, me, ch).wait_recv()

        def halo_tile(g, carry):
            lanes = pl.ds(pl.multiple_of(g * LANES, LANES), LANES)
            which = iota((MED, LANES), 1) // GW
            xh = hbuf[:, lanes]
            for k in range(8):
                rhs[0, k * LANES:(k + 1) * LANES, 0:LANES] = xh * (which == k).astype(BF16)
            out = dot(tmat[g, LANES:2 * LANES, :], rhs[0, :, 0:LANES])
            local[0:MED, lanes] = local[0:MED, lanes] + out
            return carry

        lax.fori_loop(0, tiles, halo_tile, 0)

    get_q.wait()
    get_gain.wait()
    settle(a3r.at[pl.ds(0, nz - 1)], r3)

    power = jnp.zeros((tokens, LANES), F32)
    wide = 2 * LANES
    same2 = ((iota((wide, wide), 0) // MODES) == (iota((wide, wide), 1) // GW)).astype(BF16)
    for g in range(tiles // 2):
        lanes = slice(g * wide, (g + 1) * wide)
        state = jnp.concatenate([a3r[2 * g, 0], a3r[2 * g + 1, 0]], axis=1)
        spread = jnp.concatenate([state] * 16, axis=0) * same2
        cross = dot(smat[:, lanes], spread)
        gated = qbuf[:, lanes].astype(F32) * (local[:, lanes] + cross)
        local[:, lanes] = gated
        sq = gated * gated
        power = power + sq[:, 0:LANES] + sq[:, LANES:wide]
    es[...] = jnp.sum(jnp.transpose(power), axis=0, keepdims=True)

    for d in order(nc):
        to = (ch + d) % nc
        copy = remote(es, er.at[ch], sx, rx, me, to)
        copy.start()
    er[ch] = es[...]

    mine_hit = (plan == me.astype(F32)).astype(F32)
    hit = jnp.sum(mine_hit, axis=1, keepdims=True)
    before = dot(tri, jnp.broadcast_to(hit, (groups, 2 * LANES)).astype(BF16))
    slot = (iota((groups, 2 * LANES), 1) // GW).astype(F32)
    wants = jnp.where(before == slot, mine_hit[:, NB:NB + 1], 0.0).astype(BF16)
    picked = jnp.zeros((MODES, 2 * LANES), F32)
    delta = ((iota((LANES, 2 * LANES), 0) % GW) == (iota((LANES, 2 * LANES), 1) % GW)).astype(F32)
    for g in range(tiles):
        rep = ((iota((LANES, groups), 0) // GW + g * 8) == iota((LANES, groups), 1)).astype(BF16)
        choose = (dot(rep, wants) * delta).astype(BF16)
        picked = picked + dot(a3r[g, 1], choose)

    @pl.when(y != ny - 1)
    def _():
        remote(row.at[0], tin, sf, rf, me, ch).wait_recv()

    tails = tin[...].astype(F32)
    for a in range(2):
        for b in range(2):
            block = swap_blocks(tails[8 * a:8 * a + 8, b * LANES:(b + 1) * LANES][None])[0]
            block = block + picked[8 * b:8 * b + 8, a * LANES:(a + 1) * LANES]
            for k in range(8):
                j = a * 8 + k
                if j < 10:
                    hand_ref[j, 8 * b:8 * b + 8, :] = block[:, k * GW:(k + 1) * GW]

    settle(a1s.at[pl.ds(0, nz - 1)], s1)
    settle(a2r.at[pl.ds(0, ny - 1)], s2)
    settle(a3s.at[pl.ds(0, nz - 1)], s3)

    @pl.when(me < last)
    def _():
        halo().wait_send()

    @pl.when(me == last)
    def _():
        settle(pk, sp)

    @pl.when(y == ny - 1)
    def _():
        settle(row.at[pl.ds(0, ny - 1)], sf)

    for g in range(tiles):
        lanes = slice(g * LANES, (g + 1) * LANES)
        local[:, lanes] = local[:, lanes] * gain_v[:, lanes]

    settle(er.at[pl.ds(0, nc - 1)], rx)
    energy = er[0]
    for i in range(1, nc):
        energy = energy + er[i]
    energy_ref[...] = energy
    settle(er.at[pl.ds(0, nc - 1)], sx)


def finish(width, gated_ref, hand_ref, energy_ref, out_hbm, hand_hbm, obuf, sem):
    tokens, channels = gated_ref.shape
    chunks = tokens // PIECE
    give = pltpu.make_async_copy(hand_ref, hand_hbm, sem.at[chunks])
    give.start()
    scale = lax.rsqrt(energy_ref[...] / width + 1e-05)
    scale = jnp.transpose(jnp.broadcast_to(scale, (LANES, tokens)))
    copies = []
    for c in range(chunks):
        rows = slice(c * PIECE, (c + 1) * PIECE)
        for g in range(channels // LANES):
            lanes = slice(g * LANES, (g + 1) * LANES)
            obuf[rows, lanes] = (gated_ref[rows, lanes] * scale[rows]).astype(BF16)
        copy = pltpu.make_async_copy(obuf.at[pl.ds(c * PIECE, PIECE)], out_hbm.at[pl.ds(c * PIECE, PIECE)], sem.at[c])
        copy.start()
        copies.append(copy)
    for copy in copies:
        copy.wait()
    give.wait()


def per_device(query_rows, key_rows, value_rows, residues, decay_rates, medium_taps, out_gain, reader_plan):
    tokens, channels = query_rows.shape
    tiles = channels // LANES
    groups = tiles * 8
    seq = lax.axis_size("seq")
    nz = math.isqrt(seq)
    ny = seq // nz
    nc = lax.axis_size("chan")
    cfg = (ny, nz, nc, tiles, tokens)
    chunks = tokens // MED
    vm = pltpu.VMEM
    dma = pltpu.SemaphoreType.DMA
    scratch = [
        vm((tokens, channels), BF16), vm((tokens, channels), BF16), vm((tokens, channels), BF16),
        vm((tokens, channels), BF16), vm((MED, channels), BF16),
        vm((MODES, groups), F32), vm((MODES, groups), F32), vm((groups, MED), F32), vm((NB + 1, groups), jnp.int32), vm((1, channels), F32),
        vm((channels, LANES), F32), vm((tiles, LANES, LANES), BF16),
        vm((MODES, channels), F32), vm((groups, LANES), F32), vm((groups, LANES), F32),
        vm((tiles, 2 * LANES, 8 * LANES), BF16), vm((tokens, channels), BF16),
        vm((2, 8 * LANES, 3 * LANES), BF16),
        vm((chunks, MODES, channels), F32),
        vm((nz, MODES, LANES), BF16), vm((nz, MODES, LANES), BF16), vm((nz, MODES, LANES), F32),
        vm((MODES, LANES), BF16), vm((ny, MODES, LANES), BF16),
        vm((nz, 2, MODES, LANES), BF16), vm((nz, 2, MODES, LANES), BF16),
        vm((NB * groups, 2 * LANES), F32), vm((nz - 1, ny, SLOTS, 2 * LANES), BF16),
        vm((ny, SLOTS, 2 * LANES), BF16), vm((SLOTS, 2 * LANES), BF16),
        vm((1, tokens), F32), vm((nc, 1, tokens), F32),
        dma((4, chunks)),
        dma, dma, dma, dma, dma, dma, dma, dma, dma, dma, dma, dma, dma, dma,
    ]
    hbm = pl.BlockSpec(memory_space=pltpu.HBM)
    vmem = pl.BlockSpec(memory_space=pltpu.VMEM)
    gated, hand, energy = pl.pallas_call(
        functools.partial(kernel, cfg),
        name="hyena",
        out_shape=(
            jax.ShapeDtypeStruct((tokens, channels), F32),
            jax.ShapeDtypeStruct((10, MODES, GW), F32),
            jax.ShapeDtypeStruct((1, tokens), F32),
        ),
        in_specs=[hbm] * 8,
        out_specs=(vmem, vmem, vmem),
        scratch_shapes=scratch,
        compiler_params=pltpu.CompilerParams(
            collective_id=0, has_side_effects=True, vmem_limit_bytes=48 * 1024 * 1024),
    )(*[pltpu.with_memory_space_constraint(a, pltpu.HBM) for a in (query_rows, key_rows, value_rows, residues.T, decay_rates.T, medium_taps, reader_plan.T, out_gain.reshape(1, channels))])
    return pl.pallas_call(
        functools.partial(finish, nc * channels),
        name="finish",
        out_shape=(
            jax.ShapeDtypeStruct((tokens, channels), BF16),
            jax.ShapeDtypeStruct((10, MODES, GW), F32),
        ),
        in_specs=[vmem] * 3,
        out_specs=(hbm, hbm),
        scratch_shapes=[vm((tokens, channels), BF16), dma((tokens // PIECE + 1,))],
        compiler_params=pltpu.CompilerParams(vmem_limit_bytes=48 * 1024 * 1024),
    )(gated, hand, energy)


def solution(mesh):
    placed = (
        P("seq", "chan"),
        P("seq", "chan"),
        P("seq", "chan"),
        P("chan", None),
        P("chan", None),
        P("chan", None),
        P("chan"),
        P("chan", None),
    )
    return jax.shard_map(
        per_device,
        mesh=mesh,
        in_specs=placed,
        out_specs=(P("seq", "chan"), P("seq", None, "chan")),
        check_vma=False,
    )
```
